32 devices in a mesh: groups: 2 (over x), seq: 8 (over z, y), inner: 2 (over core).
Axes of the slice: x: 2, y: 2, z: 4, core: 2. Of those that a mesh axis runs over, the one named last changes fastest.
Arguments:
- queries: bfloat16 [8192, 2048], P(('groups', 'seq', 'inner')), parts along dimension 0, may hold values from -6 to 6
- key_vectors: bfloat16 [8192, 2048], P(('groups', 'seq', 'inner')), parts along dimension 0, may hold values from -6 to 6
- value_vectors: bfloat16 [8192, 2048], P(('groups', 'seq', 'inner')), parts along dimension 0, may hold values from -6 to 6
- cache_state: float32 [8, 16, 128, 128], P('groups', 'inner'), parts along dimension 0, may hold values from -0.375 to 0.375
- prefix_lengths: int32 [8], P('groups'), parts along dimension 0, may hold values from 0 to 1024
- new_lengths: int32 [8], P('groups'), parts along dimension 0, may hold values from 1 to 3072, 4096 in all
- out_gain: float32 [2048], replicated, may hold values from 0.5 to 1.5
Outputs:
- attended: bfloat16 [8192, 2048], P(('groups', 'seq', 'inner')), parts along dimension 0
The draws below stay inside these ranges and needn't reach their ends.
There are 2 independent parts, one for each index of `groups`. The reference program is written for one: setup_inputs(seed, part) draws one part's arguments, and reference() takes and returns one part's arrays. A program takes and returns all parts, laid end to end along the dimension named above; an argument that names none is the same for every part. Nothing has to cross between parts.
Inputs may be any that keep to these rules, and one draw needn't show every extreme that they name: `new_lengths`: every prompt has at least one new token and the largest has exactly 3072; the lengths sum to 4096.
All inputs are finite; a program needn't handle non-finite values.
Results may differ from the reference program's by a relative error of at most 0.0055.
Values sent between devices are 32-bit elements; how exact they have to be, the bound alone decides.
A program may use at most 128 MiB of HBM per device.

```python
import math
import jax
import jax.numpy as jnp
import numpy as np
from jax import lax

H = 16
DK = 128
D = 2048
TOK_DEV = 256
PROMPTS = 4
TOKENS = 4096
PREFIX_MOST = 1024
SPAN_MOST = 3072


def place_ends(drawn, stream_key, smallest, top_value):
    place = [jax.random.randint(jax.random.fold_in(stream_key, axis), (), 0, length) for axis, length in enumerate(drawn.shape)]
    longest = drawn.shape.index(max(drawn.shape))
    beside = place[:longest] + [(place[longest] + 1) % drawn.shape[longest]] + place[longest + 1:]
    return drawn.at[tuple(place)].set(smallest).at[tuple(beside)].set(top_value)


def block_scale(stream_key, shape, shards, low, top_value):
    gain = 1.0
    for position, blocks in shards:
        steps = jax.random.uniform(jax.random.fold_in(jax.random.fold_in(stream_key, 6), position), (blocks,), jnp.float32, low / len(shards), top_value / len(shards))
        gain = gain * jnp.repeat(jnp.exp(steps), shape[position] // blocks).reshape((-1,) + (1,) * (len(shape) - 1 - position))
    return gain


def split_up(number_of, total, bound, lean):
    portions = [(1 << 20) // math.isqrt(grade ** lean) + 1 for grade in range(2, number_of + 1)]
    surplus, holding = total - bound - (number_of - 1), [1] * (number_of - 1)
    while surplus > 0:
        movable = [i for i in range(number_of - 1) if holding[i] < bound]
        mass, budget = sum([portions[i] for i in movable]), surplus
        for i in movable:
            addition = min(bound - holding[i], max(1, budget * portions[i] // mass), surplus)
            holding[i] = holding[i] + addition
            surplus = surplus - addition
    return np.array([bound] + holding)


def uneven(key, amount, total, bound, lean):
    if amount == 2:
        one = jax.random.randint(key, (), max(1, total - bound), min(bound, total - 1) + 1)
        return jnp.stack([one, total - one])
    sizes = jnp.asarray(split_up(amount, total, bound, lean), jnp.int32)
    twos = (amount - 1) // 2
    giver, taker = sizes[1:1 + 2 * twos:2], sizes[2:2 + 2 * twos:2]
    margin = jnp.minimum(giver - 1, bound - taker)
    moved = jax.random.randint(jax.random.fold_in(key, 1), (twos,), 0, 1 << 20) % (margin + 1)
    sizes = sizes.at[1:1 + 2 * twos:2].set(giver - moved).at[2:2 + 2 * twos:2].set(taker + moved)
    return sizes[jax.random.permutation(jax.random.fold_in(key, 2), amount)]


def gaussian(rng, dims, scale, reach, cuts=(), kind=jnp.bfloat16):
    loudness = block_scale(rng, dims, cuts, -0.22, 0.18) if cuts else 1.0
    result = jax.random.normal(rng, dims, jnp.float32) * scale * loudness
    return jnp.minimum(jnp.maximum(result, -reach), reach).astype(kind)


def setup_inputs(seed: int = 0, part: int = 0) -> dict:
    key_of = jax.random.split(jax.random.key(seed), 8)
    own_keys = jax.random.split(jax.random.fold_in(key_of[7], part), 8)
    return {
        "queries": gaussian(own_keys[0], (TOKENS, D), 1.0, 6.0, ((0, 16),)),
        "key_vectors": gaussian(own_keys[1], (TOKENS, D), 1.0, 6.0, ((0, 16),)),
        "value_vectors": gaussian(own_keys[2], (TOKENS, D), 1.0, 6.0, ((0, 16),)),
        "cache_state": gaussian(own_keys[3], (PROMPTS, H, DK, DK), (2.0 / PREFIX_MOST ** 0.5), 0.375, ((1, 2),), jnp.float32),
        "prefix_lengths": place_ends(jax.random.randint(own_keys[4], (PROMPTS,), 0, PREFIX_MOST + 1), jax.random.fold_in(own_keys[4], 1), 0, PREFIX_MOST).astype(jnp.int32),
        "new_lengths": uneven(own_keys[5], PROMPTS, TOKENS, SPAN_MOST, 1).astype(jnp.int32),
        "out_gain": jnp.clip(1.0 + 0.1 * jax.random.normal(key_of[6], (D,), jnp.float32), 0.5, 1.5),
    }


def features(entries):
    values_f = entries.astype(jnp.float32)
    return jnp.where(values_f > 0, values_f + 1.0, jnp.exp(jnp.minimum(values_f, 0.0))).astype(jnp.bfloat16)

def reference(queries, key_vectors, value_vectors, cache_state, prefix_lengths, new_lengths, out_gain):
    num_blocks = TOKENS // TOK_DEV
    query_feat = features(queries).reshape(num_blocks, TOK_DEV, H, DK)
    key_feat = features(key_vectors).reshape(num_blocks, TOK_DEV, H, DK)
    value_rows = value_vectors.reshape(num_blocks, TOK_DEV, H, DK)
    starts = (jnp.cumsum(new_lengths) - new_lengths).astype(jnp.int32)
    positions = jnp.arange(TOKENS, dtype=jnp.int32).reshape(num_blocks, TOK_DEV)
    segment = (lax.optimization_barrier(jnp.sum((positions[:, :, None] >= starts[None, None, :]).astype(jnp.int32), axis=2)) - 1).astype(jnp.int32)
    initial = prefix_lengths.astype(jnp.float32)[:, None, None, None] * cache_state
    row_ids = jnp.arange(TOK_DEV, dtype=jnp.int32)
    causal = row_ids[:, None] >= row_ids[None, :]
    prompt_ids = jnp.arange(PROMPTS, dtype=jnp.int32)

    def advance(carried, block_data):
        query_blk, key_blk, value_blk, segment_blk = block_data
        onehot = (segment_blk[None, :] == prompt_ids[:, None]).astype(jnp.float32)
        same = (segment_blk[:, None] == segment_blk[None, :]) & causal
        scores = jnp.einsum('thd,shd->hts', query_blk.astype(jnp.float32), key_blk.astype(jnp.float32))
        scores = jnp.where(same[None], scores, 0.0).astype(jnp.bfloat16)
        within = jnp.einsum('hts,she->the', scores.astype(jnp.float32), value_blk.astype(jnp.float32))
        across = jnp.einsum('pthd,phde->the', onehot[:, :, None, None] * query_blk.astype(jnp.float32), carried, precision=lax.Precision.HIGHEST)
        update = jnp.einsum('pthd,the->phde', onehot[:, :, None, None] * key_blk.astype(jnp.float32), value_blk.astype(jnp.float32))
        return (carried + update, across + within)
    final_state, mixed = lax.scan(advance, initial, (query_feat, key_feat, value_rows, segment))
    mixed = mixed.reshape(TOKENS, H, DK)
    normed = mixed / jnp.sqrt(lax.optimization_barrier(jnp.mean(mixed * mixed, axis=2, keepdims=True)) + 1e-06)
    return (normed.reshape(TOKENS, H * DK) * out_gain).astype(jnp.bfloat16)
```

```python
import functools
import math
import jax
import jax.numpy as jnp
from jax import lax
from jax.experimental import pallas as pl
from jax.experimental.pallas import tpu as pltpu
from jax.sharding import PartitionSpec as P

H = 16
DK = 128
VMEM = pltpu.VMEM
MESH = pl.DeviceIdType.MESH


def features(entries):
    values_f = entries.astype(jnp.float32)
    return jnp.where(values_f > 0, values_f + 1.0, jnp.exp(jnp.minimum(values_f, 0.0))).astype(
        jnp.bfloat16
    )


def prompt_starts(lengths_ref, prompts):
    starts, total = [], jnp.int32(0)
    for p in range(prompts):
        starts.append(total)
        total = total + lengths_ref[p]
    return starts


def no_start(starts, low, high):
    clear = jnp.float32(1.0)
    for start in starts:
        clear = clear * jnp.where((start >= low) & (start < high), 0.0, 1.0)
    return clear


def own_state_kernel(prompts, rows, lengths_ref, block_ref, k_ref, v_ref, out_ref):
    starts = prompt_starts(lengths_ref, prompts)
    first_row = block_ref[0] * rows
    last_start = jnp.int32(0)
    for start in starts:
        last_start = jnp.maximum(last_start, jnp.where(start < first_row + rows, start, 0))
    keep = (lax.broadcasted_iota(jnp.int32, (rows, DK), 0) + first_row) >= last_start
    for h in range(H):
        cols = slice(h * DK, (h + 1) * DK)
        key_feat = features(k_ref[:, cols])
        key_feat = jnp.where(keep, key_feat, jnp.zeros_like(key_feat))
        out_ref[h] = lax.dot_general(
            key_feat, v_ref[:, cols], (((0,), (0,)), ((), ())), preferred_element_type=jnp.float32
        )


def scan_kernel(
    A, B, prompts, rows, lengths_ref, own_ref, cache_ref, carry_ref, got_ref,
    pair_buf, x_buf, row_buf, z_in, z_out, back_buf,
    pair_s, pair_r, row_s, row_r, z_s, z_r, back_s, back_r, cache_s, cache_r,
):
    half = pair_buf.shape[0]
    s = lax.axis_index("seq")
    c = lax.axis_index("inner")
    other = 1 - c
    a, b = s // B, s % B
    first, last = a == 0, a == A - 1
    barrier = pltpu.get_barrier_semaphore()

    def greet(device):
        pl.semaphore_signal(barrier, inc=1, device_id=device, device_id_type=MESH)

    greet({"inner": other})
    mates = [a * B + (b + k) % B for k in range(1, B)]
    for mate in mates:
        greet({"seq": mate})
    pl.when(jnp.logical_not(first))(lambda: greet({"seq": s - B}))
    pl.when(jnp.logical_not(last))(lambda: greet({"seq": s + B}))
    ends = first.astype(jnp.int32) + last.astype(jnp.int32)
    pl.semaphore_wait(barrier, B + 2 - ends)

    def remote(src, dst, send, recv, device):
        return pltpu.make_async_remote_copy(
            src_ref=src, dst_ref=dst, send_sem=send, recv_sem=recv,
            device_id=device, device_id_type=MESH,
        )

    pair = [
        remote(own_ref.at[other * half + h], pair_buf.at[h], pair_s.at[h], pair_r.at[h], {"inner": other})
        for h in range(half)
    ]
    row = [
        [
            remote(x_buf.at[h], row_buf.at[k, h], row_s.at[k, h], row_r.at[k, h], {"seq": mates[k]})
            for k in range(B - 1)
        ]
        for h in range(half)
    ]
    down = [
        remote(z_out.at[h], z_in.at[h], z_s.at[h], z_r.at[h], {"seq": jnp.minimum(s + B, A * B - 1)})
        for h in range(half)
    ]
    back = [
        remote(back_buf.at[h], carry_ref.at[c * half + h], back_s.at[h], back_r.at[h], {"inner": other})
        for h in range(half)
    ]
    cached = remote(cache_ref, got_ref, cache_s, cache_r, {"inner": other})

    for h in range(half):
        pair[h].start()
    cached.start()

    @pl.when(first)
    def _():
        z_in[...] = jnp.zeros_like(z_in)

    starts = prompt_starts(lengths_ref, prompts)
    pair_rows = 2 * rows
    here = s * pair_rows
    row_begin, row_end = a * B * pair_rows, (a + 1) * B * pair_rows
    is_zero = jnp.where(c == 0, 1.0, 0.0).astype(jnp.float32)
    is_one = 1.0 - is_zero
    keep_zero = no_start(starts, here, here + rows)
    keep_one = no_start(starts, here + rows, here + pair_rows)
    mine_weight = is_one + is_zero * keep_one
    theirs_weight = is_zero + is_one * keep_one
    total_weights, prefix_weights = [], []
    for k in range(B):
        whose = (b + B - k) % B
        end = (a * B + whose + 1) * pair_rows
        total_weights.append(no_start(starts, end, row_end))
        prefix_weights.append(no_start(starts, end, here) * jnp.where(whose < b, 1.0, 0.0))
    keep_row = no_start(starts, row_begin, row_end)
    keep_prefix = no_start(starts, row_begin, here)

    for h in range(half):
        pair[h].wait_recv()
        x_buf[h] = mine_weight * own_ref[c * half + h] + theirs_weight * pair_buf[h]
        for copy in row[h]:
            copy.start()
    for h in range(half):
        for copy in row[h]:
            copy.wait_recv()
        total = total_weights[0] * x_buf[h]
        prefix = jnp.zeros_like(total)
        for k in range(1, B):
            got = row_buf[k - 1, h]
            total = total + total_weights[k] * got
            prefix = prefix + prefix_weights[k] * got
        pl.when(jnp.logical_not(first))(down[h].wait_recv)
        incoming = z_in[h]
        z_out[h] = total + keep_row * incoming
        pl.when(jnp.logical_not(last))(down[h].start)
        at_zero = prefix + keep_prefix * incoming
        mine, theirs = own_ref[c * half + h], pair_buf[h]
        at_one = is_zero * mine + is_one * theirs + keep_zero * at_zero
        back_buf[h] = is_one * at_zero + is_zero * at_one
        back[h].start()
        carry_ref[c * half + h] = is_zero * at_zero + is_one * at_one
    for h in range(half):
        pair[h].wait_send()
        for copy in row[h]:
            copy.wait_send()
        pl.when(jnp.logical_not(last))(down[h].wait_send)
        back[h].wait()
    cached.wait()


def attend_kernel(
    prompts, rows, info_ref, lengths_ref, prefix_ref, q_ref, k_ref, v_ref, carry_ref, near_ref,
    far_ref, gain_ref, out_ref, acc_ref,
):
    half = pl.num_programs(0) // 2
    near = pl.program_id(0) < half
    starts = prompt_starts(lengths_ref, prompts)
    first_row = info_ref[0] * rows
    down = lax.broadcasted_iota(jnp.int32, (rows, rows), 0) + first_row
    along = lax.broadcasted_iota(jnp.int32, (rows, rows), 1) + first_row
    column = lax.broadcasted_iota(jnp.int32, (rows, DK), 0) + first_row
    segment_down = jnp.full((rows, rows), -1, jnp.int32)
    segment_along = segment_down
    segment = jnp.full((rows, DK), -1, jnp.int32)
    first_segment, first_start = jnp.int32(-1), jnp.int32(0)
    for start in starts:
        segment_down = segment_down + (down >= start).astype(jnp.int32)
        segment_along = segment_along + (along >= start).astype(jnp.int32)
        segment = segment + (column >= start).astype(jnp.int32)
        reached = start <= first_row
        first_segment = first_segment + reached.astype(jnp.int32)
        first_start = jnp.where(reached, start, first_start)
    mask = (segment_down == segment_along) & (down >= along)
    query_feat = features(q_ref[...])
    key_feat = features(k_ref[...])
    scores = lax.dot_general(
        query_feat, key_feat, (((1,), (1,)), ((), ())), preferred_element_type=jnp.float32
    )
    scores = jnp.where(mask, scores, 0.0).astype(jnp.bfloat16)
    acc_ref[...] = jnp.dot(scores, v_ref[...], preferred_element_type=jnp.float32)

    def apply(state):
        upper = state.astype(jnp.bfloat16)
        lower = (state - upper.astype(jnp.float32)).astype(jnp.bfloat16)
        return jnp.dot(query_feat, upper, preferred_element_type=jnp.float32) + jnp.dot(
            query_feat, lower, preferred_element_type=jnp.float32
        )

    def cached(p):
        state = jnp.where(near, near_ref[p, 0], far_ref[p, 0])
        return prefix_ref[p].astype(jnp.float32) * state

    use_carry = jnp.where(first_start < first_row, 1.0, 0.0).astype(jnp.float32)
    state = cached(first_segment) + use_carry * carry_ref[0]
    acc_ref[...] += jnp.where(segment == first_segment, apply(state), 0.0)
    for p in range(1, prompts):

        @pl.when((starts[p] > first_row) & (starts[p] < first_row + rows))
        def _():
            acc_ref[...] += jnp.where(segment == p, apply(cached(p)), 0.0)

    mixed = acc_ref[...]
    scale = 1.0 / jnp.sqrt(jnp.mean(mixed * mixed, axis=1, keepdims=True) + 1e-06)
    out_ref[...] = (mixed * scale * gain_ref[...]).astype(jnp.bfloat16)


def on_device(
    count, queries, key_vectors, value_vectors, cache_state, prefix_lengths, new_lengths, out_gain
):
    rows, width = queries.shape
    prompts = new_lengths.shape[0]
    half = H // 2
    block_index = lax.axis_index(("seq", "inner")).astype(jnp.int32)
    inner = lax.axis_index("inner").astype(jnp.int32)
    block_vec = block_index[None]
    vmem = pl.BlockSpec(memory_space=VMEM)
    smem = pl.BlockSpec(memory_space=pltpu.SMEM)
    anywhere = pl.BlockSpec(memory_space=pl.ANY)
    state_shape = jax.ShapeDtypeStruct((H, DK, DK), jnp.float32)
    own = pl.pallas_call(
        functools.partial(own_state_kernel, prompts, rows),
        out_shape=state_shape,
        in_specs=[smem, smem, vmem, vmem],
        out_specs=vmem,
        name="own_state",
    )(new_lengths, block_vec, key_vectors, value_vectors)

    B = max(d for d in range(1, math.isqrt(count) + 1) if count % d == 0)
    A = count // B
    part = (half, DK, DK)
    sems = lambda *shape: pltpu.SemaphoreType.DMA(shape)
    carry, far = pl.pallas_call(
        functools.partial(scan_kernel, A, B, prompts, rows),
        out_shape=(state_shape, jax.ShapeDtypeStruct(cache_state.shape, jnp.float32)),
        in_specs=[smem, vmem, anywhere],
        out_specs=(vmem, anywhere),
        scratch_shapes=[
            VMEM(part, jnp.float32), VMEM(part, jnp.float32),
            VMEM((B - 1,) + part, jnp.float32),
            VMEM(part, jnp.float32), VMEM(part, jnp.float32), VMEM(part, jnp.float32),
            sems(half), sems(half), sems(B - 1, half), sems(B - 1, half),
            sems(half), sems(half), sems(half), sems(half),
            pltpu.SemaphoreType.DMA, pltpu.SemaphoreType.DMA,
        ],
        compiler_params=pltpu.CompilerParams(collective_id=0, has_side_effects=True),
        name="state_scan",
    )(new_lengths, own, cache_state)

    def head(g, info):
        mine = info[1]
        return jnp.where(g < half, mine * half + g, (1 - mine) * half + g - half)

    cols = lambda g, info, *_: (0, head(g, info))
    return pl.pallas_call(
        functools.partial(attend_kernel, prompts, rows),
        out_shape=jax.ShapeDtypeStruct((rows, width), jnp.bfloat16),
        grid_spec=pltpu.PrefetchScalarGridSpec(
            num_scalar_prefetch=3,
            grid=(H,),
            in_specs=[
                pl.BlockSpec((rows, DK), cols),
                pl.BlockSpec((rows, DK), cols),
                pl.BlockSpec((rows, DK), cols),
                pl.BlockSpec((1, DK, DK), lambda g, info, *_: (head(g, info), 0, 0)),
                pl.BlockSpec((prompts, 1, DK, DK), lambda g, *_: (0, jnp.minimum(g, half - 1), 0, 0)),
                pl.BlockSpec((prompts, 1, DK, DK), lambda g, *_: (0, jnp.maximum(g - half, 0), 0, 0)),
                pl.BlockSpec((1, DK), cols),
            ],
            out_specs=pl.BlockSpec((rows, DK), cols),
            scratch_shapes=[VMEM((rows, DK), jnp.float32)],
        ),
        name="attend",
    )(
        jnp.stack([block_index, inner]), new_lengths, prefix_lengths,
        queries, key_vectors, value_vectors, carry, cache_state, far, out_gain[None, :],
    )


def solution(mesh):
    in_specs = (
        P(("groups", "seq", "inner"), None),
        P(("groups", "seq", "inner"), None),
        P(("groups", "seq", "inner"), None),
        P("groups", "inner", None, None),
        P("groups"),
        P("groups"),
        P(),
    )
    out_specs = P(("groups", "seq", "inner"), None)
    return jax.shard_map(
        functools.partial(on_device, mesh.shape["seq"]),
        mesh=mesh, in_specs=in_specs, out_specs=out_specs, check_vma=False,
    )
```

```python
import functools
import math
import jax
import jax.numpy as jnp
from jax import lax
from jax.experimental import pallas as pl
from jax.experimental.pallas import tpu as pltpu
from jax.sharding import PartitionSpec as P

H = 16
DK = 128
VMEM = pltpu.VMEM
MESH = pl.DeviceIdType.MESH


def features(entries):
    values_f = entries.astype(jnp.float32)
    return jnp.where(values_f > 0, values_f + 1.0, jnp.exp(jnp.minimum(values_f, 0.0))).astype(
        jnp.bfloat16
    )


def prompt_starts(lengths_ref, prompts):
    starts, total = [], jnp.int32(0)
    for p in range(prompts):
        starts.append(total)
        total = total + lengths_ref[p]
    return starts


def no_start(starts, low, high):
    clear = jnp.float32(1.0)
    for start in starts:
        clear = clear * jnp.where((start >= low) & (start < high), 0.0, 1.0)
    return clear


def layer_kernel(
    A, B, lengths_ref, prefix_ref, k_ref, v_ref, gain_ref, q_hbm, cache_hbm, out_ref,
    q_ref, near_ref, far_ref, key_ref, carry_query_ref, acc_ref, own_ref, carry_ref, mask_ref,
    prompt_mask_ref, carry_mask_ref,
    pair_buf, x_buf, row_buf, z_in, z_out, back_buf,
    pair_s, pair_r, row_s, row_r, z_s, z_r, back_s, back_r, far_s, far_r, near_sem, q_sem,
):
    half = pair_buf.shape[0]
    rows = k_ref.shape[0]
    prompts = near_ref.shape[0]
    s = lax.axis_index("seq")
    c = lax.axis_index("inner")
    other = 1 - c
    a, b = s // B, s % B
    first, last = a == 0, a == A - 1
    barrier = pltpu.get_barrier_semaphore()

    def greet(device):
        pl.semaphore_signal(barrier, inc=1, device_id=device, device_id_type=MESH)

    greet({"inner": other})
    mates = [a * B + (b + k) % B for k in range(1, B)]
    for mate in mates:
        greet({"seq": mate})
    pl.when(jnp.logical_not(first))(lambda: greet({"seq": s - B}))
    pl.when(jnp.logical_not(last))(lambda: greet({"seq": s + B}))

    def remote(src, dst, send, recv, device):
        return pltpu.make_async_remote_copy(
            src_ref=src, dst_ref=dst, send_sem=send, recv_sem=recv,
            device_id=device, device_id_type=MESH,
        )

    def pair(h):
        return remote(
            own_ref.at[other * half + h], pair_buf.at[h], pair_s.at[h], pair_r.at[h],
            {"inner": other},
        )

    def row(h):
        return [
            remote(x_buf.at[h], row_buf.at[k, h], row_s.at[k, h], row_r.at[k, h], {"seq": mates[k]})
            for k in range(B - 1)
        ]

    def down(h):
        return remote(
            z_out.at[h], z_in.at[h], z_s.at[h], z_r.at[h], {"seq": jnp.minimum(s + B, A * B - 1)}
        )

    def back(h):
        return remote(
            back_buf.at[h], carry_ref.at[c * half + h], back_s.at[h], back_r.at[h],
            {"inner": other},
        )

    near_copy = pltpu.make_async_copy(cache_hbm, near_ref, near_sem)
    q_copy = pltpu.make_async_copy(q_hbm, q_ref, q_sem)
    far_copy = remote(cache_hbm, far_ref, far_s, far_r, {"inner": other})
    q_copy.start()
    near_copy.start()

    starts = prompt_starts(lengths_ref, prompts)
    pair_rows = 2 * rows
    here = s * pair_rows
    first_row = here + c * rows
    row_begin, row_end = a * B * pair_rows, (a + 1) * B * pair_rows
    is_zero = jnp.where(c == 0, 1.0, 0.0).astype(jnp.float32)
    is_one = 1.0 - is_zero
    keep_zero = no_start(starts, here, here + rows)
    keep_one = no_start(starts, here + rows, here + pair_rows)
    mine_weight = is_one + is_zero * keep_one
    theirs_weight = is_zero + is_one * keep_one
    total_weights, prefix_weights = [], []
    for k in range(B):
        whose = (b + B - k) % B
        end = (a * B + whose + 1) * pair_rows
        total_weights.append(no_start(starts, end, row_end))
        prefix_weights.append(no_start(starts, end, here) * jnp.where(whose < b, 1.0, 0.0))
    keep_row = no_start(starts, row_begin, row_end)
    keep_prefix = no_start(starts, row_begin, here)

    last_start, first_start = jnp.int32(0), jnp.int32(0)
    for start in starts:
        last_start = jnp.maximum(last_start, jnp.where(start < first_row + rows, start, 0))
        first_start = jnp.maximum(first_start, jnp.where(start <= first_row, start, 0))
    column = lax.broadcasted_iota(jnp.int32, (rows, DK), 0) + first_row
    in_last = column >= last_start

    def columns(head):
        return pl.ds(pl.multiple_of(head * DK, DK), DK)

    def own_state(head):
        cols = columns(head)
        key_feat = features(k_ref[:, cols])
        key_ref[:, cols] = key_feat
        key_feat = jnp.where(in_last, key_feat, jnp.zeros_like(key_feat))
        own_ref[head] = lax.dot_general(
            key_feat, v_ref[:, cols], (((0,), (0,)), ((), ())), preferred_element_type=jnp.float32
        )

    ends = first.astype(jnp.int32) + last.astype(jnp.int32)
    pl.semaphore_wait(barrier, B + 2 - ends)

    @pl.loop(0, half)
    def _(h):
        own_state(other * half + h)
        pair(h).start()

    far_copy.start()

    @pl.loop(0, half)
    def _(h):
        own_state(c * half + h)
        pair(h).wait_recv()
        x_buf[h] = mine_weight * own_ref[c * half + h] + theirs_weight * pair_buf[h]
        for copy in row(h):
            copy.start()

    @pl.when(first)
    def _():
        z_in[...] = jnp.zeros_like(z_in)

    segment_down = lax.broadcasted_iota(jnp.int32, (rows, rows), 0) + first_row
    segment_along = lax.broadcasted_iota(jnp.int32, (rows, rows), 1) + first_row
    mask = segment_down >= segment_along
    for start in starts:
        mask = mask & ((segment_down < start) | (segment_along >= start))
    mask_ref[...] = jnp.where(mask, 1.0, 0.0)
    for p in range(prompts):
        inside = column >= starts[p]
        if p + 1 < prompts:
            inside = inside & (column < starts[p + 1])
        prompt_mask_ref[p] = jnp.where(inside, 1.0, 0.0).astype(jnp.bfloat16)
    after = jnp.int32(2**31 - 1)
    for start in starts:
        after = jnp.minimum(after, jnp.where(start > first_row, start, after))
    carried = (column < after) & (first_start < first_row)
    carry_mask_ref[...] = jnp.where(carried, 1.0, 0.0).astype(jnp.bfloat16)
    near_copy.wait()
    q_copy.wait()
    far_copy.wait()

    def split(state):
        upper = state.astype(jnp.bfloat16)
        return upper, (state - upper.astype(jnp.float32)).astype(jnp.bfloat16)

    def local_terms(cached, head, h):
        cols = columns(head)
        query_feat = features(q_ref[:, cols])
        carry_query_ref[:, cols] = query_feat * carry_mask_ref[...]
        scores = lax.dot_general(
            query_feat, key_ref[:, cols], (((1,), (1,)), ((), ())),
            preferred_element_type=jnp.float32,
        )
        scores = (scores * mask_ref[...]).astype(jnp.bfloat16)
        acc = jnp.dot(scores, v_ref[:, cols], preferred_element_type=jnp.float32)
        uppers, lowers, queries = [], [], []
        for p in range(prompts):
            upper, lower = split(prefix_ref[p].astype(jnp.float32) * cached[p, h])
            uppers.append(upper)
            lowers.append(lower)
            queries.append(query_feat * prompt_mask_ref[p])
        masked = jnp.concatenate(queries, axis=1)
        acc += jnp.dot(masked, jnp.concatenate(uppers, 0), preferred_element_type=jnp.float32)
        acc += jnp.dot(masked, jnp.concatenate(lowers, 0), preferred_element_type=jnp.float32)
        acc_ref[:, cols] = acc

    def both_local(h):
        local_terms(near_ref, c * half + h, h)
        local_terms(far_ref, other * half + h, h)

    def finish(head):
        cols = columns(head)
        query = carry_query_ref[:, cols]
        state = jnp.concatenate(split(carry_ref[head]), axis=0)
        mixed = acc_ref[:, cols] + jnp.dot(
            jnp.concatenate([query, query], axis=1), state, preferred_element_type=jnp.float32
        )
        scale = 1.0 / jnp.sqrt(jnp.mean(mixed * mixed, axis=1, keepdims=True) + 1e-06)
        out_ref[:, cols] = (mixed * scale * gain_ref[:, cols]).astype(jnp.bfloat16)

    def both_finish(h):
        back(h).wait_recv()
        finish(c * half + h)
        finish(other * half + h)

    ahead = (half * a) // max(A - 1, 1)

    @pl.loop(0, ahead)
    def _(h):
        both_local(h)

    late = a >= A // 2

    @pl.loop(0, half)
    def _(h):
        for copy in row(h):
            copy.wait_recv()
        total = total_weights[0] * x_buf[h]
        prefix = jnp.zeros_like(total)
        for k in range(1, B):
            got = row_buf[k - 1, h]
            total = total + total_weights[k] * got
            prefix = prefix + prefix_weights[k] * got
        pl.when(jnp.logical_not(first))(lambda: down(h).wait_recv())
        incoming = z_in[h]
        z_out[h] = total + keep_row * incoming
        pl.when(jnp.logical_not(last))(lambda: down(h).start())
        at_zero = prefix + keep_prefix * incoming
        mine, theirs = own_ref[c * half + h], pair_buf[h]
        at_one = is_zero * mine + is_one * theirs + keep_zero * at_zero
        back_buf[h] = is_one * at_zero + is_zero * at_one
        back(h).start()
        carry_ref[c * half + h] = is_zero * at_zero + is_one * at_one
        pl.when(h >= ahead)(lambda: both_local(h))
        pl.when(late & (h > 0))(lambda: both_finish(h - 1))

    @pl.loop(jnp.where(late, half - 1, 0), half)
    def _(h):
        both_finish(h)

    @pl.loop(0, half)
    def _(h):
        pair(h).wait_send()
        for copy in row(h):
            copy.wait_send()
        pl.when(jnp.logical_not(last))(lambda: down(h).wait_send())
        back(h).wait_send()


def on_device(
    count, queries, key_vectors, value_vectors, cache_state, prefix_lengths, new_lengths, out_gain
):
    rows, width = queries.shape
    prompts, half = cache_state.shape[:2]
    vmem = pl.BlockSpec(memory_space=VMEM)
    smem = pl.BlockSpec(memory_space=pltpu.SMEM)
    anywhere = pl.BlockSpec(memory_space=pl.ANY)
    B = max(d for d in range(1, math.isqrt(count) + 1) if count % d == 0)
    A = count // B
    f32, bf16 = jnp.float32, jnp.bfloat16
    part = VMEM((half, DK, DK), f32)
    whole = VMEM((2 * half, DK, DK), f32)
    cache = VMEM(cache_state.shape, f32)
    sems = lambda *shape: pltpu.SemaphoreType.DMA(shape)
    return pl.pallas_call(
        functools.partial(layer_kernel, A, B),
        out_shape=jax.ShapeDtypeStruct((rows, width), bf16),
        in_specs=[smem, smem, vmem, vmem, vmem, anywhere, anywhere],
        out_specs=vmem,
        scratch_shapes=[
            VMEM((rows, width), bf16), cache, cache, VMEM((rows, width), bf16),
            VMEM((rows, width), bf16), VMEM((rows, width), f32), whole, whole,
            VMEM((rows, rows), f32), VMEM((prompts, rows, DK), bf16), VMEM((rows, DK), bf16),
            part, part, VMEM((B - 1, half, DK, DK), f32), part, part, part,
            sems(half), sems(half), sems(B - 1, half), sems(B - 1, half),
            sems(half), sems(half), sems(half), sems(half),
            pltpu.SemaphoreType.DMA, pltpu.SemaphoreType.DMA,
            pltpu.SemaphoreType.DMA, pltpu.SemaphoreType.DMA,
        ],
        compiler_params=pltpu.CompilerParams(collective_id=0, has_side_effects=True),
        name="layer",
    )(
        new_lengths, prefix_lengths, key_vectors, value_vectors, out_gain[None, :],
        queries, cache_state,
    )


def solution(mesh):
    in_specs = (
        P(("groups", "seq", "inner"), None),
        P(("groups", "seq", "inner"), None),
        P(("groups", "seq", "inner"), None),
        P("groups", "inner", None, None),
        P("groups"),
        P("groups"),
        P(),
    )
    out_specs = P(("groups", "seq", "inner"), None)
    return jax.shard_map(
        functools.partial(on_device, mesh.shape["seq"]),
        mesh=mesh, in_specs=in_specs, out_specs=out_specs, check_vma=False,
    )
```

```python
import functools
import math
import jax
import jax.numpy as jnp
from jax import lax
from jax.experimental import pallas as pl
from jax.experimental.pallas import tpu as pltpu
from jax.sharding import PartitionSpec as P

H = 16
DK = 128
VMEM = pltpu.VMEM
MESH = pl.DeviceIdType.MESH


def features(entries):
    values_f = entries.astype(jnp.float32)
    return jnp.where(values_f > 0, values_f + 1.0, jnp.exp(jnp.minimum(values_f, 0.0))).astype(
        jnp.bfloat16
    )


def prompt_starts(lengths_ref, prompts):
    starts, total = [], jnp.int32(0)
    for p in range(prompts):
        starts.append(total)
        total = total + lengths_ref[p]
    return starts


def no_start(starts, low, high):
    clear = jnp.float32(1.0)
    for start in starts:
        clear = clear * jnp.where((start >= low) & (start < high), 0.0, 1.0)
    return clear


def layer_kernel(
    A, B, lengths_ref, prefix_ref, k_ref, v_ref, gain_ref, q_hbm, cache_hbm, out_ref,
    q_ref, cached_ref, key_ref, carry_query_ref, acc_ref, own_ref, carry_ref, mask_ref,
    prompt_mask_ref, carry_mask_ref,
    pair_buf, x_buf, row_buf, z_in, z_out, back_buf,
    pair_s, pair_r, row_s, row_r, z_s, z_r, back_s, back_r, far_s, far_r, near_sem, q_sem,
):
    half = pair_buf.shape[0]
    rows = k_ref.shape[0]
    prompts = cached_ref.shape[1]
    chunk_rows = DK // 2
    chunks = 2 * half
    s = lax.axis_index("seq")
    c = lax.axis_index("inner")
    other = 1 - c
    a, b = s // B, s % B
    first, last = a == 0, a == A - 1
    barrier = pltpu.get_barrier_semaphore()

    def greet(device):
        pl.semaphore_signal(barrier, inc=1, device_id=device, device_id_type=MESH)

    greet({"inner": other})
    mates = [a * B + (b + k) % B for k in range(1, B)]
    for mate in mates:
        greet({"seq": mate})
    pl.when(jnp.logical_not(first))(lambda: greet({"seq": s - B}))
    pl.when(jnp.logical_not(last))(lambda: greet({"seq": s + B}))

    def remote(src, dst, send, recv, device):
        return pltpu.make_async_remote_copy(
            src_ref=src, dst_ref=dst, send_sem=send, recv_sem=recv,
            device_id=device, device_id_type=MESH,
        )

    def pair(h):
        return remote(
            own_ref.at[other * half + h], pair_buf.at[h], pair_s.at[h], pair_r.at[h],
            {"inner": other},
        )

    def piece(ref, head, u):
        return ref.at[head, pl.ds(pl.multiple_of(u * chunk_rows, chunk_rows), chunk_rows)]

    def row(h, u):
        j = 2 * h + u
        return [
            remote(
                piece(x_buf, h, u), piece(row_buf.at[k], h, u), row_s.at[k, j], row_r.at[k, j],
                {"seq": mates[k]},
            )
            for k in range(B - 1)
        ]

    def down(h, u):
        j = 2 * h + u
        return remote(
            piece(z_out, h, u), piece(z_in, h, u), z_s.at[j], z_r.at[j],
            {"seq": jnp.minimum(s + B, A * B - 1)},
        )

    def back(h, u):
        j = 2 * h + u
        return remote(
            piece(back_buf, h, u), piece(carry_ref, c * half + h, u), back_s.at[j], back_r.at[j],
            {"inner": other},
        )

    near_copy = pltpu.make_async_copy(cache_hbm, cached_ref.at[0], near_sem)
    q_copy = pltpu.make_async_copy(q_hbm, q_ref, q_sem)
    far_copy = remote(cache_hbm, cached_ref.at[1], far_s, far_r, {"inner": other})
    q_copy.start()
    near_copy.start()

    starts = prompt_starts(lengths_ref, prompts)
    pair_rows = 2 * rows
    here = s * pair_rows
    first_row = here + c * rows
    row_begin, row_end = a * B * pair_rows, (a + 1) * B * pair_rows
    is_zero = jnp.where(c == 0, 1.0, 0.0).astype(jnp.float32)
    is_one = 1.0 - is_zero
    keep_zero = no_start(starts, here, here + rows)
    keep_one = no_start(starts, here + rows, here + pair_rows)
    mine_weight = is_one + is_zero * keep_one
    theirs_weight = is_zero + is_one * keep_one
    total_weights, prefix_weights = [], []
    for k in range(B):
        whose = (b + B - k) % B
        end = (a * B + whose + 1) * pair_rows
        total_weights.append(no_start(starts, end, row_end))
        prefix_weights.append(no_start(starts, end, here) * jnp.where(whose < b, 1.0, 0.0))
    keep_row = no_start(starts, row_begin, row_end)
    keep_prefix = no_start(starts, row_begin, here)

    last_start, first_start = jnp.int32(0), jnp.int32(0)
    for start in starts:
        last_start = jnp.maximum(last_start, jnp.where(start < first_row + rows, start, 0))
        first_start = jnp.maximum(first_start, jnp.where(start <= first_row, start, 0))
    column = lax.broadcasted_iota(jnp.int32, (rows, DK), 0) + first_row
    in_last = column >= last_start

    def columns(head):
        return pl.ds(pl.multiple_of(head * DK, DK), DK)

    def own_state(head):
        cols = columns(head)
        key_feat = features(k_ref[:, cols])
        key_ref[:, cols] = key_feat
        key_feat = jnp.where(in_last, key_feat, jnp.zeros_like(key_feat))
        own_ref[head] = lax.dot_general(
            key_feat, v_ref[:, cols], (((0,), (0,)), ((), ())), preferred_element_type=jnp.float32
        )

    def spread(h):
        pair(h).wait_recv()
        x_buf[h] = mine_weight * own_ref[c * half + h] + theirs_weight * pair_buf[h]
        for u in range(2):
            for copy in row(h, u):
                copy.start()

    own_state(other * half)
    ends = first.astype(jnp.int32) + last.astype(jnp.int32)
    pl.semaphore_wait(barrier, B + 2 - ends)
    pair(0).start()
    own_state(c * half)

    @pl.loop(1, half)
    def _(h):
        own_state(other * half + h)
        pair(h).start()
        own_state(c * half + h)
        spread(h - 1)

    far_copy.start()
    spread(half - 1)

    @pl.when(first)
    def _():
        z_in[...] = jnp.zeros_like(z_in)

    segment_down = lax.broadcasted_iota(jnp.int32, (rows, rows), 0) + first_row
    segment_along = lax.broadcasted_iota(jnp.int32, (rows, rows), 1) + first_row
    mask = segment_down >= segment_along
    for start in starts:
        mask = mask & ((segment_down < start) | (segment_along >= start))
    mask_ref[...] = jnp.where(mask, 1.0, 0.0)
    for p in range(prompts):
        inside = column >= starts[p]
        if p + 1 < prompts:
            inside = inside & (column < starts[p + 1])
        prompt_mask_ref[p] = jnp.where(inside, 1.0, 0.0).astype(jnp.bfloat16)
    after = jnp.int32(2**31 - 1)
    for start in starts:
        after = jnp.minimum(after, jnp.where(start > first_row, start, after))
    carried = (column < after) & (first_start < first_row)
    carry_mask_ref[...] = jnp.where(carried, 1.0, 0.0).astype(jnp.bfloat16)
    near_copy.wait()
    q_copy.wait()
    far_copy.wait()

    def split(state):
        upper = state.astype(jnp.bfloat16)
        return upper, (state - upper.astype(jnp.float32)).astype(jnp.bfloat16)

    def local_terms(h, side):
        head = jnp.where(side == 0, c, other) * half + h
        cols = columns(head)
        query_feat = features(q_ref[:, cols])
        carry_query_ref[:, cols] = query_feat * carry_mask_ref[...]
        scores = lax.dot_general(
            query_feat, key_ref[:, cols], (((1,), (1,)), ((), ())),
            preferred_element_type=jnp.float32,
        )
        scores = (scores * mask_ref[...]).astype(jnp.bfloat16)
        acc = jnp.dot(scores, v_ref[:, cols], preferred_element_type=jnp.float32)
        uppers, lowers, queries = [], [], []
        for p in range(prompts):
            upper, lower = split(prefix_ref[p].astype(jnp.float32) * cached_ref[side, p, h])
            uppers.append(upper)
            lowers.append(lower)
            queries.append(query_feat * prompt_mask_ref[p])
        masked = jnp.concatenate(queries, axis=1)
        acc += jnp.dot(masked, jnp.concatenate(uppers, 0), preferred_element_type=jnp.float32)
        acc += jnp.dot(masked, jnp.concatenate(lowers, 0), preferred_element_type=jnp.float32)
        acc_ref[:, cols] = acc

    def finish(head):
        cols = columns(head)
        query = carry_query_ref[:, cols]
        state = jnp.concatenate(split(carry_ref[head]), axis=0)
        mixed = acc_ref[:, cols] + jnp.dot(
            jnp.concatenate([query, query], axis=1), state, preferred_element_type=jnp.float32
        )
        scale = 1.0 / jnp.sqrt(jnp.mean(mixed * mixed, axis=1, keepdims=True) + 1e-06)
        out_ref[:, cols] = (mixed * scale * gain_ref[:, cols]).astype(jnp.bfloat16)

    def unit(i):
        @pl.when(i < chunks)
        def _():
            local_terms(i // 2, i % 2)

        @pl.when(i >= chunks)
        def _():
            h, side = (i - chunks) // 2, i % 2

            @pl.when(side == 0)
            def _():
                back(h, 0).wait_recv()
                back(h, 1).wait_recv()

            finish(jnp.where(side == 0, c, other) * half + h)

    ahead = (chunks * a) // max(A - 1, 1)
    late = a >= A // 2

    def done(j):
        full = jnp.maximum(ahead, jnp.minimum(ahead + j, chunks + j - 4))
        return jnp.where(late, full, ahead + j // 2)

    pl.loop(0, ahead)(unit)

    @pl.loop(0, chunks)
    def _(j):
        h, u = j // 2, j % 2
        part = pl.ds(pl.multiple_of(u * chunk_rows, chunk_rows), chunk_rows)
        for copy in row(h, u):
            copy.wait_recv()
        total = total_weights[0] * x_buf[h, part]
        prefix = jnp.zeros_like(total)
        for k in range(1, B):
            got = row_buf[k - 1, h, part]
            total = total + total_weights[k] * got
            prefix = prefix + prefix_weights[k] * got
        pl.when(jnp.logical_not(first))(lambda: down(h, u).wait_recv())
        incoming = z_in[h, part]
        z_out[h, part] = total + keep_row * incoming
        pl.when(jnp.logical_not(last))(lambda: down(h, u).start())
        at_zero = prefix + keep_prefix * incoming
        mine, theirs = own_ref[c * half + h, part], pair_buf[h, part]
        at_one = is_zero * mine + is_one * theirs + keep_zero * at_zero
        back_buf[h, part] = is_one * at_zero + is_zero * at_one
        back(h, u).start()
        carry_ref[c * half + h, part] = is_zero * at_zero + is_one * at_one
        pl.loop(done(j), done(j + 1))(unit)

    pl.loop(done(chunks), 2 * chunks)(unit)

    @pl.loop(0, half)
    def _(h):
        pair(h).wait_send()
        for u in range(2):
            for copy in row(h, u):
                copy.wait_send()
            pl.when(jnp.logical_not(last))(lambda: down(h, u).wait_send())
            back(h, u).wait_send()


def on_device(
    count, queries, key_vectors, value_vectors, cache_state, prefix_lengths, new_lengths, out_gain
):
    rows, width = queries.shape
    prompts, half = cache_state.shape[:2]
    vmem = pl.BlockSpec(memory_space=VMEM)
    smem = pl.BlockSpec(memory_space=pltpu.SMEM)
    anywhere = pl.BlockSpec(memory_space=pl.ANY)
    B = max(d for d in range(1, math.isqrt(count) + 1) if count % d == 0)
    A = count // B
    f32, bf16 = jnp.float32, jnp.bfloat16
    part = VMEM((half, DK, DK), f32)
    whole = VMEM((2 * half, DK, DK), f32)
    sems = lambda *shape: pltpu.SemaphoreType.DMA(shape)
    return pl.pallas_call(
        functools.partial(layer_kernel, A, B),
        out_shape=jax.ShapeDtypeStruct((rows, width), bf16),
        in_specs=[smem, smem, vmem, vmem, vmem, anywhere, anywhere],
        out_specs=vmem,
        scratch_shapes=[
            VMEM((rows, width), bf16), VMEM((2,) + cache_state.shape, f32), VMEM((rows, width), bf16),
            VMEM((rows, width), bf16), VMEM((rows, width), f32), whole, whole,
            VMEM((rows, rows), f32), VMEM((prompts, rows, DK), bf16), VMEM((rows, DK), bf16),
            part, part, VMEM((B - 1, half, DK, DK), f32), part, part, part,
            sems(half), sems(half), sems(B - 1, 2 * half), sems(B - 1, 2 * half),
            sems(2 * half), sems(2 * half), sems(2 * half), sems(2 * half),
            pltpu.SemaphoreType.DMA, pltpu.SemaphoreType.DMA,
            pltpu.SemaphoreType.DMA, pltpu.SemaphoreType.DMA,
        ],
        compiler_params=pltpu.CompilerParams(collective_id=0, has_side_effects=True),
        name="layer",
    )(
        new_lengths, prefix_lengths, key_vectors, value_vectors, out_gain[None, :],
        queries, cache_state,
    )


def solution(mesh):
    in_specs = (
        P(("groups", "seq", "inner"), None),
        P(("groups", "seq", "inner"), None),
        P(("groups", "seq", "inner"), None),
        P("groups", "inner", None, None),
        P("groups"),
        P("groups"),
        P(),
    )
    out_specs = P(("groups", "seq", "inner"), None)
    return jax.shard_map(
        functools.partial(on_device, mesh.shape["seq"]),
        mesh=mesh, in_specs=in_specs, out_specs=out_specs, check_vma=False,
    )
```

```python
import functools
import math
import jax
import jax.numpy as jnp
from jax import lax
from jax.experimental import pallas as pl
from jax.experimental.pallas import tpu as pltpu
from jax.sharding import PartitionSpec as P

H = 16
DK = 128
VMEM = pltpu.VMEM
MESH = pl.DeviceIdType.MESH


def features(entries):
    values_f = entries.astype(jnp.float32)
    return jnp.where(values_f > 0, values_f + 1.0, jnp.exp(jnp.minimum(values_f, 0.0))).astype(
        jnp.bfloat16
    )


def prompt_starts(lengths_ref, prompts):
    starts, total = [], jnp.int32(0)
    for p in range(prompts):
        starts.append(total)
        total = total + lengths_ref[p]
    return starts


def no_start(starts, low, high):
    clear = jnp.float32(1.0)
    for start in starts:
        clear = clear * jnp.where((start >= low) & (start < high), 0.0, 1.0)
    return clear


def layer_kernel(
    A, B, lengths_ref, prefix_ref, k_ref, v_ref, gain_ref, q_hbm, cache_hbm, out_ref,
    q_ref, cached_ref, key_ref, carry_query_ref, acc_ref, own_ref, carry_ref, mask_ref,
    prompt_mask_ref, carry_mask_ref,
    pair_buf, x_buf, row_buf, z_in, z_out, back_buf,
    pair_s, pair_r, row_s, row_r, z_s, z_r, back_s, back_r, far_s, far_r, near_sem, q_sem,
):
    half = pair_buf.shape[0]
    rows = k_ref.shape[0]
    prompts = cached_ref.shape[1]
    chunk_rows = DK // 2
    s = lax.axis_index("seq")
    c = lax.axis_index("inner")
    other = 1 - c
    a, b = s // B, s % B
    first, last = a == 0, a == A - 1
    barrier = pltpu.get_barrier_semaphore()

    def greet(device):
        pl.semaphore_signal(barrier, inc=1, device_id=device, device_id_type=MESH)

    greet({"inner": other})
    mates = [a * B + (b + k) % B for k in range(1, B)]
    for mate in mates:
        greet({"seq": mate})
    pl.when(jnp.logical_not(first))(lambda: greet({"seq": s - B}))
    pl.when(jnp.logical_not(last))(lambda: greet({"seq": s + B}))

    def remote(src, dst, send, recv, device):
        return pltpu.make_async_remote_copy(
            src_ref=src, dst_ref=dst, send_sem=send, recv_sem=recv,
            device_id=device, device_id_type=MESH,
        )

    def pair(h):
        return remote(
            own_ref.at[other * half + h], pair_buf.at[h], pair_s.at[h], pair_r.at[h],
            {"inner": other},
        )

    def piece(ref, head, u):
        return ref.at[head, pl.ds(u * chunk_rows, chunk_rows)]

    def row(h, u):
        j = 2 * h + u
        return [
            remote(
                piece(x_buf, h, u), piece(row_buf.at[k], h, u), row_s.at[k, j], row_r.at[k, j],
                {"seq": mates[k]},
            )
            for k in range(B - 1)
        ]

    def down(h, u):
        j = 2 * h + u
        return remote(
            piece(z_out, h, u), piece(z_in, h, u), z_s.at[j], z_r.at[j],
            {"seq": jnp.minimum(s + B, A * B - 1)},
        )

    def back(h, u):
        j = 2 * h + u
        return remote(
            piece(back_buf, h, u), piece(carry_ref, c * half + h, u), back_s.at[j], back_r.at[j],
            {"inner": other},
        )

    near_copy = pltpu.make_async_copy(cache_hbm, cached_ref.at[0], near_sem)
    q_copy = pltpu.make_async_copy(q_hbm, q_ref, q_sem)
    far_copy = remote(cache_hbm, cached_ref.at[1], far_s, far_r, {"inner": other})
    q_copy.start()
    near_copy.start()

    starts = prompt_starts(lengths_ref, prompts)
    pair_rows = 2 * rows
    here = s * pair_rows
    first_row = here + c * rows
    row_begin, row_end = a * B * pair_rows, (a + 1) * B * pair_rows
    is_zero = jnp.where(c == 0, 1.0, 0.0).astype(jnp.float32)
    is_one = 1.0 - is_zero
    keep_zero = no_start(starts, here, here + rows)
    keep_one = no_start(starts, here + rows, here + pair_rows)
    mine_weight = is_one + is_zero * keep_one
    theirs_weight = is_zero + is_one * keep_one
    total_weights, prefix_weights = [], []
    for k in range(B):
        whose = (b + B - k) % B
        end = (a * B + whose + 1) * pair_rows
        total_weights.append(no_start(starts, end, row_end))
        prefix_weights.append(no_start(starts, end, here) * jnp.where(whose < b, 1.0, 0.0))
    keep_row = no_start(starts, row_begin, row_end)
    keep_prefix = no_start(starts, row_begin, here)

    last_start, first_start = jnp.int32(0), jnp.int32(0)
    for start in starts:
        last_start = jnp.maximum(last_start, jnp.where(start < first_row + rows, start, 0))
        first_start = jnp.maximum(first_start, jnp.where(start <= first_row, start, 0))
    column = lax.broadcasted_iota(jnp.int32, (rows, DK), 0) + first_row
    in_last = column >= last_start

    def columns(head):
        return pl.ds(pl.multiple_of(head * DK, DK), DK)

    def own_state(head):
        cols = columns(head)
        key_feat = features(k_ref[:, cols])
        key_ref[:, cols] = key_feat
        key_feat = jnp.where(in_last, key_feat, jnp.zeros_like(key_feat))
        own_ref[head] = lax.dot_general(
            key_feat, v_ref[:, cols], (((0,), (0,)), ((), ())), preferred_element_type=jnp.float32
        )

    def spread(h):
        pair(h).wait_recv()
        x_buf[h] = mine_weight * own_ref[c * half + h] + theirs_weight * pair_buf[h]
        for u in range(2):
            for copy in row(h, u):
                copy.start()

    own_state(other * half)
    ends = first.astype(jnp.int32) + last.astype(jnp.int32)
    pl.semaphore_wait(barrier, B + 2 - ends)
    pair(0).start()
    own_state(c * half)

    @pl.loop(1, half)
    def _(h):
        own_state(other * half + h)
        pair(h).start()
        own_state(c * half + h)
        spread(h - 1)

    far_copy.start()
    spread(half - 1)

    @pl.when(first)
    def _():
        z_in[...] = jnp.zeros_like(z_in)

    segment_down = lax.broadcasted_iota(jnp.int32, (rows, rows), 0) + first_row
    segment_along = lax.broadcasted_iota(jnp.int32, (rows, rows), 1) + first_row
    mask = segment_down >= segment_along
    for start in starts:
        mask = mask & ((segment_down < start) | (segment_along >= start))
    mask_ref[...] = jnp.where(mask, 1.0, 0.0)
    for p in range(prompts):
        inside = column >= starts[p]
        if p + 1 < prompts:
            inside = inside & (column < starts[p + 1])
        prompt_mask_ref[p] = jnp.where(inside, 1.0, 0.0).astype(jnp.bfloat16)
    after = jnp.int32(2**31 - 1)
    for start in starts:
        after = jnp.minimum(after, jnp.where(start > first_row, start, after))
    carried = (column < after) & (first_start < first_row)
    carry_mask_ref[...] = jnp.where(carried, 1.0, 0.0).astype(jnp.bfloat16)
    near_copy.wait()
    q_copy.wait()
    far_copy.wait()

    def split(state):
        upper = state.astype(jnp.bfloat16)
        return upper, (state - upper.astype(jnp.float32)).astype(jnp.bfloat16)

    def local_terms(h, side):
        head = (other if side else c) * half + h
        cols = columns(head)
        query_feat = features(q_ref[:, cols])
        carry_query_ref[:, cols] = query_feat * carry_mask_ref[...]
        scores = lax.dot_general(
            query_feat, key_ref[:, cols], (((1,), (1,)), ((), ())),
            preferred_element_type=jnp.float32,
        )
        scores = (scores * mask_ref[...]).astype(jnp.bfloat16)
        acc = jnp.dot(scores, v_ref[:, cols], preferred_element_type=jnp.float32)
        uppers, lowers, queries = [], [], []
        for p in range(prompts):
            upper, lower = split(prefix_ref[p].astype(jnp.float32) * cached_ref[side, p, h])
            uppers.append(upper)
            lowers.append(lower)
            queries.append(query_feat * prompt_mask_ref[p])
        masked = jnp.concatenate(queries, axis=1)
        acc += jnp.dot(masked, jnp.concatenate(uppers, 0), preferred_element_type=jnp.float32)
        acc += jnp.dot(masked, jnp.concatenate(lowers, 0), preferred_element_type=jnp.float32)
        acc_ref[:, cols] = acc

    def finish(head):
        cols = columns(head)
        query = carry_query_ref[:, cols]
        state = jnp.concatenate(split(carry_ref[head]), axis=0)
        mixed = acc_ref[:, cols] + jnp.dot(
            jnp.concatenate([query, query], axis=1), state, preferred_element_type=jnp.float32
        )
        scale = 1.0 / jnp.sqrt(jnp.mean(mixed * mixed, axis=1, keepdims=True) + 1e-06)
        out_ref[:, cols] = (mixed * scale * gain_ref[:, cols]).astype(jnp.bfloat16)

    def both_local(h):
        local_terms(h, 0)
        local_terms(h, 1)

    def both_finish(h):
        back(h, 0).wait_recv()
        back(h, 1).wait_recv()
        finish(c * half + h)
        finish(other * half + h)

    ahead = (half * a + A // 2) // max(A - 1, 1)
    late = a >= A // 2
    pl.loop(0, ahead)(both_local)

    @pl.loop(0, half)
    def _(h):
        for u in range(2):
            part = pl.ds(u * chunk_rows, chunk_rows)
            for copy in row(h, u):
                copy.wait_recv()
            total = total_weights[0] * x_buf[h, part]
            prefix = jnp.zeros_like(total)
            for k in range(1, B):
                got = row_buf[k - 1, h, part]
                total = total + total_weights[k] * got
                prefix = prefix + prefix_weights[k] * got
            pl.when(jnp.logical_not(first))(lambda: down(h, u).wait_recv())
            incoming = z_in[h, part]
            z_out[h, part] = total + keep_row * incoming
            pl.when(jnp.logical_not(last))(lambda: down(h, u).start())
            at_zero = prefix + keep_prefix * incoming
            mine, theirs = own_ref[c * half + h, part], pair_buf[h, part]
            at_one = is_zero * mine + is_one * theirs + keep_zero * at_zero
            back_buf[h, part] = is_one * at_zero + is_zero * at_one
            back(h, u).start()
            carry_ref[c * half + h, part] = is_zero * at_zero + is_one * at_one
        pl.when(h >= ahead)(lambda: both_local(h))
        pl.when(late & (h > 0))(lambda: both_finish(h - 1))

    pl.loop(jnp.where(late, half - 1, 0), half)(both_finish)

    @pl.loop(0, half)
    def _(h):
        pair(h).wait_send()
        for u in range(2):
            for copy in row(h, u):
                copy.wait_send()
            pl.when(jnp.logical_not(last))(lambda: down(h, u).wait_send())
            back(h, u).wait_send()


def on_device(
    count, queries, key_vectors, value_vectors, cache_state, prefix_lengths, new_lengths, out_gain
):
    rows, width = queries.shape
    prompts, half = cache_state.shape[:2]
    vmem = pl.BlockSpec(memory_space=VMEM)
    smem = pl.BlockSpec(memory_space=pltpu.SMEM)
    anywhere = pl.BlockSpec(memory_space=pl.ANY)
    B = max(d for d in range(1, math.isqrt(count) + 1) if count % d == 0)
    A = count // B
    f32, bf16 = jnp.float32, jnp.bfloat16
    part = VMEM((half, DK, DK), f32)
    whole = VMEM((2 * half, DK, DK), f32)
    sems = lambda *shape: pltpu.SemaphoreType.DMA(shape)
    return pl.pallas_call(
        functools.partial(layer_kernel, A, B),
        out_shape=jax.ShapeDtypeStruct((rows, width), bf16),
        in_specs=[smem, smem, vmem, vmem, vmem, anywhere, anywhere],
        out_specs=vmem,
        scratch_shapes=[
            VMEM((rows, width), bf16), VMEM((2,) + cache_state.shape, f32), VMEM((rows, width), bf16),
            VMEM((rows, width), bf16), VMEM((rows, width), f32), whole, whole,
            VMEM((rows, rows), f32), VMEM((prompts, rows, DK), bf16), VMEM((rows, DK), bf16),
            part, part, VMEM((B - 1, half, DK, DK), f32), part, part, part,
            sems(half), sems(half), sems(B - 1, 2 * half), sems(B - 1, 2 * half),
            sems(2 * half), sems(2 * half), sems(2 * half), sems(2 * half),
            pltpu.SemaphoreType.DMA, pltpu.SemaphoreType.DMA,
            pltpu.SemaphoreType.DMA, pltpu.SemaphoreType.DMA,
        ],
        compiler_params=pltpu.CompilerParams(collective_id=0, has_side_effects=True),
        name="layer",
    )(
        new_lengths, prefix_lengths, key_vectors, value_vectors, out_gain[None, :],
        queries, cache_state,
    )


def solution(mesh):
    in_specs = (
        P(("groups", "seq", "inner"), None),
        P(("groups", "seq", "inner"), None),
        P(("groups", "seq", "inner"), None),
        P("groups", "inner", None, None),
        P("groups"),
        P("groups"),
        P(),
    )
    out_specs = P(("groups", "seq", "inner"), None)
    return jax.shard_map(
        functools.partial(on_device, mesh.shape["seq"]),
        mesh=mesh, in_specs=in_specs, out_specs=out_specs, check_vma=False,
    )
```

```python
import functools
import math
import jax
import jax.numpy as jnp
from jax import lax
from jax.experimental import pallas as pl
from jax.experimental.pallas import tpu as pltpu
from jax.sharding import PartitionSpec as P

H = 16
DK = 128
VMEM = pltpu.VMEM
MESH = pl.DeviceIdType.MESH


def features(entries):
    values_f = entries.astype(jnp.float32)
    return jnp.where(values_f > 0, values_f + 1.0, jnp.exp(jnp.minimum(values_f, 0.0))).astype(
        jnp.bfloat16
    )


def prompt_starts(lengths_ref, prompts):
    starts, total = [], jnp.int32(0)
    for p in range(prompts):
        starts.append(total)
        total = total + lengths_ref[p]
    return starts


def no_start(starts, low, high):
    clear = jnp.float32(1.0)
    for start in starts:
        clear = clear * jnp.where((start >= low) & (start < high), 0.0, 1.0)
    return clear


def layer_kernel(
    A, B, lengths_ref, prefix_ref, k_ref, v_ref, gain_ref, q_hbm, cache_hbm, out_ref,
    q_ref, cached_ref, key_ref, carry_query_ref, acc_ref, own_ref, carry_ref, mask_ref,
    prompt_mask_ref, carry_mask_ref,
    pair_buf, x_buf, row_buf, z_in, z_out, back_buf,
    pair_s, pair_r, row_s, row_r, z_s, z_r, back_s, back_r, far_s, far_r, near_sem, q_sem,
):
    half = pair_buf.shape[0]
    rows = k_ref.shape[0]
    prompts = cached_ref.shape[1]
    chunk_rows = DK // 2
    s = lax.axis_index("seq")
    c = lax.axis_index("inner")
    other = 1 - c
    a, b = s // B, s % B
    first, last = a == 0, a == A - 1
    barrier = pltpu.get_barrier_semaphore()

    def greet(device):
        pl.semaphore_signal(barrier, inc=1, device_id=device, device_id_type=MESH)

    greet({"inner": other})
    mates = [a * B + (b + k) % B for k in range(1, B)]
    for mate in mates:
        greet({"seq": mate})
    pl.when(jnp.logical_not(first))(lambda: greet({"seq": s - B}))
    pl.when(jnp.logical_not(last))(lambda: greet({"seq": s + B}))

    def remote(src, dst, send, recv, device):
        return pltpu.make_async_remote_copy(
            src_ref=src, dst_ref=dst, send_sem=send, recv_sem=recv,
            device_id=device, device_id_type=MESH,
        )

    def pair(h):
        return remote(
            own_ref.at[other * half + h], pair_buf.at[h], pair_s.at[h], pair_r.at[h],
            {"inner": other},
        )

    def piece(ref, head, u):
        return ref.at[head, pl.ds(u * chunk_rows, chunk_rows)]

    def row(h, u):
        j = 2 * h + u
        return [
            remote(
                piece(x_buf, h, u), piece(row_buf.at[k], h, u), row_s.at[k, j], row_r.at[k, j],
                {"seq": mates[k]},
            )
            for k in range(B - 1)
        ]

    def down(h, u):
        j = 2 * h + u
        return remote(
            piece(z_out, h, u), piece(z_in, h, u), z_s.at[j], z_r.at[j],
            {"seq": jnp.minimum(s + B, A * B - 1)},
        )

    def back(h, u):
        j = 2 * h + u
        return remote(
            piece(back_buf, h, u), piece(carry_ref, c * half + h, u), back_s.at[j], back_r.at[j],
            {"inner": other},
        )

    near_copy = pltpu.make_async_copy(cache_hbm, cached_ref.at[0], near_sem)
    q_copy = pltpu.make_async_copy(q_hbm, q_ref, q_sem)

    def far(h):
        return remote(
            cache_hbm.at[:, h], cached_ref.at[1, :, h], far_s.at[h], far_r.at[h], {"inner": other}
        )

    q_copy.start()
    near_copy.start()

    starts = prompt_starts(lengths_ref, prompts)
    pair_rows = 2 * rows
    here = s * pair_rows
    first_row = here + c * rows
    row_begin, row_end = a * B * pair_rows, (a + 1) * B * pair_rows
    is_zero = jnp.where(c == 0, 1.0, 0.0).astype(jnp.float32)
    is_one = 1.0 - is_zero
    keep_zero = no_start(starts, here, here + rows)
    keep_one = no_start(starts, here + rows, here + pair_rows)
    mine_weight = is_one + is_zero * keep_one
    theirs_weight = is_zero + is_one * keep_one
    total_weights, prefix_weights = [], []
    for k in range(B):
        whose = (b + B - k) % B
        end = (a * B + whose + 1) * pair_rows
        total_weights.append(no_start(starts, end, row_end))
        prefix_weights.append(no_start(starts, end, here) * jnp.where(whose < b, 1.0, 0.0))
    keep_row = no_start(starts, row_begin, row_end)
    keep_prefix = no_start(starts, row_begin, here)

    last_start, first_start = jnp.int32(0), jnp.int32(0)
    for start in starts:
        last_start = jnp.maximum(last_start, jnp.where(start < first_row + rows, start, 0))
        first_start = jnp.maximum(first_start, jnp.where(start <= first_row, start, 0))
    column = lax.broadcasted_iota(jnp.int32, (rows, DK), 0) + first_row
    in_last = column >= last_start

    def columns(head):
        return pl.ds(pl.multiple_of(head * DK, DK), DK)

    def own_state(head):
        cols = columns(head)
        key_feat = features(k_ref[:, cols])
        key_ref[:, cols] = key_feat
        key_feat = jnp.where(in_last, key_feat, jnp.zeros_like(key_feat))
        own_ref[head] = lax.dot_general(
            key_feat, v_ref[:, cols], (((0,), (0,)), ((), ())), preferred_element_type=jnp.float32
        )

    def spread(h):
        pair(h).wait_recv()
        x_buf[h] = mine_weight * own_ref[c * half + h] + theirs_weight * pair_buf[h]
        for u in range(2):
            for copy in row(h, u):
                copy.start()

    own_state(other * half)
    ends = first.astype(jnp.int32) + last.astype(jnp.int32)
    pl.semaphore_wait(barrier, B + 2 - ends)
    pair(0).start()
    far(0).start()
    own_state(c * half)

    @pl.loop(1, half)
    def _(h):
        own_state(other * half + h)
        pair(h).start()
        far(h).start()
        own_state(c * half + h)
        spread(h - 1)

    spread(half - 1)

    @pl.when(first)
    def _():
        z_in[...] = jnp.zeros_like(z_in)

    segment_down = lax.broadcasted_iota(jnp.int32, (rows, rows), 0) + first_row
    segment_along = lax.broadcasted_iota(jnp.int32, (rows, rows), 1) + first_row
    mask = segment_down >= segment_along
    for start in starts:
        mask = mask & ((segment_down < start) | (segment_along >= start))
    mask_ref[...] = jnp.where(mask, 1.0, 0.0)
    for p in range(prompts):
        inside = column >= starts[p]
        if p + 1 < prompts:
            inside = inside & (column < starts[p + 1])
        prompt_mask_ref[p] = jnp.where(inside, 1.0, 0.0).astype(jnp.bfloat16)
    after = jnp.int32(2**31 - 1)
    for start in starts:
        after = jnp.minimum(after, jnp.where(start > first_row, start, after))
    carried = (column < after) & (first_start < first_row)
    carry_mask_ref[...] = jnp.where(carried, 1.0, 0.0).astype(jnp.bfloat16)
    near_copy.wait()
    q_copy.wait()

    def split(state):
        upper = state.astype(jnp.bfloat16)
        return upper, (state - upper.astype(jnp.float32)).astype(jnp.bfloat16)

    def local_terms(h, side):
        head = (other if side else c) * half + h
        cols = columns(head)
        query_feat = features(q_ref[:, cols])
        carry_query_ref[:, cols] = query_feat * carry_mask_ref[...]
        scores = lax.dot_general(
            query_feat, key_ref[:, cols], (((1,), (1,)), ((), ())),
            preferred_element_type=jnp.float32,
        )
        scores = (scores * mask_ref[...]).astype(jnp.bfloat16)
        acc = jnp.dot(scores, v_ref[:, cols], preferred_element_type=jnp.float32)
        uppers, lowers, queries = [], [], []
        for p in range(prompts):
            upper, lower = split(prefix_ref[p].astype(jnp.float32) * cached_ref[side, p, h])
            uppers.append(upper)
            lowers.append(lower)
            queries.append(query_feat * prompt_mask_ref[p])
        masked = jnp.concatenate(queries, axis=1)
        acc += jnp.dot(masked, jnp.concatenate(uppers, 0), preferred_element_type=jnp.float32)
        acc += jnp.dot(masked, jnp.concatenate(lowers, 0), preferred_element_type=jnp.float32)
        acc_ref[:, cols] = acc

    def finish(head):
        cols = columns(head)
        query = carry_query_ref[:, cols]
        state = jnp.concatenate(split(carry_ref[head]), axis=0)
        mixed = acc_ref[:, cols] + jnp.dot(
            jnp.concatenate([query, query], axis=1), state, preferred_element_type=jnp.float32
        )
        scale = 1.0 / jnp.sqrt(jnp.mean(mixed * mixed, axis=1, keepdims=True) + 1e-06)
        out_ref[:, cols] = (mixed * scale * gain_ref[:, cols]).astype(jnp.bfloat16)

    def both_local(h):
        far(h).wait_recv()
        local_terms(h, 0)
        local_terms(h, 1)

    def both_finish(h):
        back(h, 0).wait_recv()
        back(h, 1).wait_recv()
        finish(c * half + h)
        finish(other * half + h)

    ahead = (half * a + A // 2) // max(A - 1, 1)
    late = a >= A // 2
    pl.loop(0, ahead)(both_local)

    @pl.loop(0, half)
    def _(h):
        for u in range(2):
            part = pl.ds(u * chunk_rows, chunk_rows)
            for copy in row(h, u):
                copy.wait_recv()
            total = total_weights[0] * x_buf[h, part]
            prefix = jnp.zeros_like(total)
            for k in range(1, B):
                got = row_buf[k - 1, h, part]
                total = total + total_weights[k] * got
                prefix = prefix + prefix_weights[k] * got
            pl.when(jnp.logical_not(first))(lambda: down(h, u).wait_recv())
            incoming = z_in[h, part]
            z_out[h, part] = total + keep_row * incoming
            pl.when(jnp.logical_not(last))(lambda: down(h, u).start())
            at_zero = prefix + keep_prefix * incoming
            mine, theirs = own_ref[c * half + h, part], pair_buf[h, part]
            at_one = is_zero * mine + is_one * theirs + keep_zero * at_zero
            back_buf[h, part] = is_one * at_zero + is_zero * at_one
            back(h, u).start()
            carry_ref[c * half + h, part] = is_zero * at_zero + is_one * at_one
        pl.when(h >= ahead)(lambda: both_local(h))
        pl.when(late & (h > 0))(lambda: both_finish(h - 1))

    pl.loop(jnp.where(late, half - 1, 0), half)(both_finish)

    @pl.loop(0, half)
    def _(h):
        pair(h).wait_send()
        far(h).wait_send()
        for u in range(2):
            for copy in row(h, u):
                copy.wait_send()
            pl.when(jnp.logical_not(last))(lambda: down(h, u).wait_send())
            back(h, u).wait_send()


def on_device(
    count, queries, key_vectors, value_vectors, cache_state, prefix_lengths, new_lengths, out_gain
):
    rows, width = queries.shape
    prompts, half = cache_state.shape[:2]
    vmem = pl.BlockSpec(memory_space=VMEM)
    smem = pl.BlockSpec(memory_space=pltpu.SMEM)
    anywhere = pl.BlockSpec(memory_space=pl.ANY)
    B = max(d for d in range(1, math.isqrt(count) + 1) if count % d == 0)
    A = count // B
    f32, bf16 = jnp.float32, jnp.bfloat16
    part = VMEM((half, DK, DK), f32)
    whole = VMEM((2 * half, DK, DK), f32)
    sems = lambda *shape: pltpu.SemaphoreType.DMA(shape)
    return pl.pallas_call(
        functools.partial(layer_kernel, A, B),
        out_shape=jax.ShapeDtypeStruct((rows, width), bf16),
        in_specs=[smem, smem, vmem, vmem, vmem, anywhere, anywhere],
        out_specs=vmem,
        scratch_shapes=[
            VMEM((rows, width), bf16), VMEM((2,) + cache_state.shape, f32), VMEM((rows, width), bf16),
            VMEM((rows, width), bf16), VMEM((rows, width), f32), whole, whole,
            VMEM((rows, rows), f32), VMEM((prompts, rows, DK), bf16), VMEM((rows, DK), bf16),
            part, part, VMEM((B - 1, half, DK, DK), f32), part, part, part,
            sems(half), sems(half), sems(B - 1, 2 * half), sems(B - 1, 2 * half),
            sems(2 * half), sems(2 * half), sems(2 * half), sems(2 * half),
            sems(half), sems(half), pltpu.SemaphoreType.DMA, pltpu.SemaphoreType.DMA,
        ],
        compiler_params=pltpu.CompilerParams(collective_id=0, has_side_effects=True),
        name="layer",
    )(
        new_lengths, prefix_lengths, key_vectors, value_vectors, out_gain[None, :],
        queries, cache_state,
    )


def solution(mesh):
    in_specs = (
        P(("groups", "seq", "inner"), None),
        P(("groups", "seq", "inner"), None),
        P(("groups", "seq", "inner"), None),
        P("groups", "inner", None, None),
        P("groups"),
        P("groups"),
        P(),
    )
    out_specs = P(("groups", "seq", "inner"), None)
    return jax.shard_map(
        functools.partial(on_device, mesh.shape["seq"]),
        mesh=mesh, in_specs=in_specs, out_specs=out_specs, check_vma=False,
    )
```

```python
import functools
import math
import jax
import jax.numpy as jnp
from jax import lax
from jax.experimental import pallas as pl
from jax.experimental.pallas import tpu as pltpu
from jax.sharding import PartitionSpec as P

H = 16
DK = 128
VMEM = pltpu.VMEM
MESH = pl.DeviceIdType.MESH


def features(entries):
    values_f = entries.astype(jnp.float32)
    return jnp.where(values_f > 0, values_f + 1.0, jnp.exp(jnp.minimum(values_f, 0.0))).astype(
        jnp.bfloat16
    )


def prompt_starts(lengths_ref, prompts):
    starts, total = [], jnp.int32(0)
    for p in range(prompts):
        starts.append(total)
        total = total + lengths_ref[p]
    return starts


def no_start(starts, low, high):
    clear = jnp.float32(1.0)
    for start in starts:
        clear = clear * jnp.where((start >= low) & (start < high), 0.0, 1.0)
    return clear


def layer_kernel(
    A, B, lengths_ref, prefix_ref, k_ref, v_ref, gain_ref, q_hbm, cache_hbm, out_ref,
    q_ref, cached_ref, key_ref, carry_query_ref, acc_ref, own_ref, carry_ref, mask_ref,
    prompt_mask_ref, carry_mask_ref,
    pair_buf, x_buf, row_buf, z_in, z_out, back_buf,
    pair_s, pair_r, row_s, row_r, z_s, z_r, back_s, back_r, far_s, far_r, near_sem, q_sem,
):
    half = pair_buf.shape[0]
    rows = k_ref.shape[0]
    prompts = cached_ref.shape[1]
    chunk_rows = DK // 2
    s = lax.axis_index("seq")
    c = lax.axis_index("inner")
    other = 1 - c
    a, b = s // B, s % B
    first, last = a == 0, a == A - 1
    barrier = pltpu.get_barrier_semaphore()

    def greet(device):
        pl.semaphore_signal(barrier, inc=1, device_id=device, device_id_type=MESH)

    greet({"inner": other})
    mates = [a * B + (b + k) % B for k in range(1, B)]
    for mate in mates:
        greet({"seq": mate})
    pl.when(jnp.logical_not(first))(lambda: greet({"seq": s - B}))
    pl.when(jnp.logical_not(last))(lambda: greet({"seq": s + B}))

    def remote(src, dst, send, recv, device):
        return pltpu.make_async_remote_copy(
            src_ref=src, dst_ref=dst, send_sem=send, recv_sem=recv,
            device_id=device, device_id_type=MESH,
        )

    def pair(h):
        return remote(
            own_ref.at[other * half + h], pair_buf.at[h], pair_s.at[h], pair_r.at[h],
            {"inner": other},
        )

    def piece(ref, head, u):
        return ref.at[head, pl.ds(u * chunk_rows, chunk_rows)]

    def row(h, u):
        j = 2 * h + u
        return [
            remote(
                piece(x_buf, h, u), piece(row_buf.at[k], h, u), row_s.at[k, j], row_r.at[k, j],
                {"seq": mates[k]},
            )
            for k in range(B - 1)
        ]

    def down(h, u):
        j = 2 * h + u
        return remote(
            piece(z_out, h, u), piece(z_in, h, u), z_s.at[j], z_r.at[j],
            {"seq": jnp.minimum(s + B, A * B - 1)},
        )

    def back(h, u):
        j = 2 * h + u
        return remote(
            piece(back_buf, h, u), piece(carry_ref, c * half + h, u), back_s.at[j], back_r.at[j],
            {"inner": other},
        )

    near_copy = pltpu.make_async_copy(cache_hbm, cached_ref.at[0], near_sem)
    q_copy = pltpu.make_async_copy(q_hbm, q_ref, q_sem)

    def far(h):
        return remote(
            cache_hbm.at[:, h], cached_ref.at[1, :, h], far_s.at[h], far_r.at[h], {"inner": other}
        )

    q_copy.start()
    near_copy.start()

    starts = prompt_starts(lengths_ref, prompts)
    pair_rows = 2 * rows
    here = s * pair_rows
    first_row = here + c * rows
    row_begin, row_end = a * B * pair_rows, (a + 1) * B * pair_rows
    is_zero = jnp.where(c == 0, 1.0, 0.0).astype(jnp.float32)
    is_one = 1.0 - is_zero
    keep_zero = no_start(starts, here, here + rows)
    keep_one = no_start(starts, here + rows, here + pair_rows)
    mine_weight = is_one + is_zero * keep_one
    theirs_weight = is_zero + is_one * keep_one
    total_weights, prefix_weights = [], []
    for k in range(B):
        whose = (b + B - k) % B
        end = (a * B + whose + 1) * pair_rows
        total_weights.append(no_start(starts, end, row_end))
        prefix_weights.append(no_start(starts, end, here) * jnp.where(whose < b, 1.0, 0.0))
    keep_row = no_start(starts, row_begin, row_end)
    keep_prefix = no_start(starts, row_begin, here)

    last_start, first_start = jnp.int32(0), jnp.int32(0)
    for start in starts:
        last_start = jnp.maximum(last_start, jnp.where(start < first_row + rows, start, 0))
        first_start = jnp.maximum(first_start, jnp.where(start <= first_row, start, 0))
    column = lax.broadcasted_iota(jnp.int32, (rows, DK), 0) + first_row
    in_last = column >= last_start

    def columns(head):
        return pl.ds(pl.multiple_of(head * DK, DK), DK)

    def own_state(head):
        cols = columns(head)
        key_feat = features(k_ref[:, cols])
        key_ref[:, cols] = key_feat
        key_feat = jnp.where(in_last, key_feat, jnp.zeros_like(key_feat))
        own_ref[head] = lax.dot_general(
            key_feat, v_ref[:, cols], (((0,), (0,)), ((), ())), preferred_element_type=jnp.float32
        )

    def spread(h):
        pair(h).wait_recv()
        x_buf[h] = mine_weight * own_ref[c * half + h] + theirs_weight * pair_buf[h]
        for u in range(2):
            for copy in row(h, u):
                copy.start()

    own_state(other * half)
    ends = first.astype(jnp.int32) + last.astype(jnp.int32)
    pl.semaphore_wait(barrier, B + 2 - ends)
    pair(0).start()
    far(0).start()
    own_state(c * half)

    @pl.loop(1, half)
    def _(h):
        own_state(other * half + h)
        pair(h).start()
        far(h).start()
        own_state(c * half + h)
        spread(h - 1)

    spread(half - 1)

    @pl.when(first)
    def _():
        z_in[...] = jnp.zeros_like(z_in)

    segment_down = lax.broadcasted_iota(jnp.int32, (rows, rows), 0) + first_row
    segment_along = lax.broadcasted_iota(jnp.int32, (rows, rows), 1) + first_row
    mask = segment_down >= segment_along
    for start in starts:
        mask = mask & ((segment_down < start) | (segment_along >= start))
    mask_ref[...] = jnp.where(mask, 1.0, 0.0)
    for p in range(prompts):
        inside = column >= starts[p]
        if p + 1 < prompts:
            inside = inside & (column < starts[p + 1])
        prompt_mask_ref[p] = jnp.where(inside, 1.0, 0.0).astype(jnp.bfloat16)
    after = jnp.int32(2**31 - 1)
    for start in starts:
        after = jnp.minimum(after, jnp.where(start > first_row, start, after))
    carried = (column < after) & (first_start < first_row)
    carry_mask_ref[...] = jnp.where(carried, 1.0, 0.0).astype(jnp.bfloat16)
    near_copy.wait()
    q_copy.wait()

    def split(state):
        upper = state.astype(jnp.bfloat16)
        return upper, (state - upper.astype(jnp.float32)).astype(jnp.bfloat16)

    def local_terms(h, side):
        head = (other if side else c) * half + h
        cols = columns(head)
        query_feat = features(q_ref[:, cols])
        carry_query_ref[:, cols] = query_feat * carry_mask_ref[...]
        scores = lax.dot_general(
            query_feat, key_ref[:, cols], (((1,), (1,)), ((), ())),
            preferred_element_type=jnp.float32,
        )
        scores = (scores * mask_ref[...]).astype(jnp.bfloat16)
        acc = jnp.dot(scores, v_ref[:, cols], preferred_element_type=jnp.float32)
        uppers, lowers, queries = [], [], []
        for p in range(prompts):
            upper, lower = split(prefix_ref[p].astype(jnp.float32) * cached_ref[side, p, h])
            uppers.append(upper)
            lowers.append(lower)
            queries.append(query_feat * prompt_mask_ref[p])
        masked = jnp.concatenate(queries, axis=1)
        acc += jnp.dot(masked, jnp.concatenate(uppers, 0), preferred_element_type=jnp.float32)
        acc += jnp.dot(masked, jnp.concatenate(lowers, 0), preferred_element_type=jnp.float32)
        acc_ref[:, cols] = acc

    def finish(head):
        cols = columns(head)
        query = carry_query_ref[:, cols]
        state = jnp.concatenate(split(carry_ref[head]), axis=0)
        mixed = acc_ref[:, cols] + jnp.dot(
            jnp.concatenate([query, query], axis=1), state, preferred_element_type=jnp.float32
        )
        scale = 1.0 / jnp.sqrt(jnp.mean(mixed * mixed, axis=1, keepdims=True) + 1e-06)
        out_ref[:, cols] = (mixed * scale * gain_ref[:, cols]).astype(jnp.bfloat16)

    def both_local(h):
        far(h).wait_recv()
        local_terms(h, 0)
        local_terms(h, 1)

    def both_finish(h):
        back(h, 0).wait_recv()
        back(h, 1).wait_recv()
        finish(c * half + h)
        finish(other * half + h)

    ahead = (half * a + A // 2) // max(A - 1, 1)
    late = a >= A // 2
    pl.loop(0, ahead)(both_local)

    @pl.loop(0, half)
    def _(h):
        for u in range(2):
            part = pl.ds(u * chunk_rows, chunk_rows)
            for copy in row(h, u):
                copy.wait_recv()
            total = total_weights[0] * x_buf[h, part]
            prefix = jnp.zeros_like(total)
            for k in range(1, B):
                got = row_buf[k - 1, h, part]
                total = total + total_weights[k] * got
                prefix = prefix + prefix_weights[k] * got
            pl.when(jnp.logical_not(first))(lambda: down(h, u).wait_recv())
            incoming = z_in[h, part]
            z_out[h, part] = total + keep_row * incoming
            pl.when(jnp.logical_not(last))(lambda: down(h, u).start())
            at_zero = prefix + keep_prefix * incoming
            mine, theirs = own_ref[c * half + h, part], pair_buf[h, part]
            at_one = is_zero * mine + is_one * theirs + keep_zero * at_zero
            back_buf[h, part] = is_one * at_zero + is_zero * at_one
            back(h, u).start()
            carry_ref[c * half + h, part] = is_zero * at_zero + is_one * at_one
        pl.when(late & (h >= ahead))(lambda: both_local(h))
        ready = ahead + h // 2
        early = jnp.logical_not(late) & (h % 2 == 1) & (ready < half)
        pl.when(early)(lambda: both_local(ready))
        pl.when(late & (h > 0))(lambda: both_finish(h - 1))

    pl.loop(jnp.where(late, half, jnp.minimum(ahead + half // 2, half)), half)(both_local)
    pl.loop(jnp.where(late, half - 1, 0), half)(both_finish)

    @pl.loop(0, half)
    def _(h):
        pair(h).wait_send()
        far(h).wait_send()
        for u in range(2):
            for copy in row(h, u):
                copy.wait_send()
            pl.when(jnp.logical_not(last))(lambda: down(h, u).wait_send())
            back(h, u).wait_send()


def deliver_kernel(in_hbm, out_hbm, buffer, in_sem, out_sem):
    pieces = in_sem.shape[0]
    size = buffer.shape[0] // pieces
    loads, stores = [], []
    for i in range(pieces):
        part = pl.ds(i * size, size)
        loads.append(pltpu.make_async_copy(in_hbm.at[part], buffer.at[part], in_sem.at[i]))
        stores.append(pltpu.make_async_copy(buffer.at[part], out_hbm.at[part], out_sem.at[i]))
    for load in loads:
        load.start()
    for load, store in zip(loads, stores):
        load.wait()
        store.start()
    for store in stores:
        store.wait()


def on_device(
    count, queries, key_vectors, value_vectors, cache_state, prefix_lengths, new_lengths, out_gain
):
    rows, width = queries.shape
    prompts, half = cache_state.shape[:2]
    vmem = pl.BlockSpec(memory_space=VMEM)
    smem = pl.BlockSpec(memory_space=pltpu.SMEM)
    anywhere = pl.BlockSpec(memory_space=pl.ANY)
    B = max(d for d in range(1, math.isqrt(count) + 1) if count % d == 0)
    A = count // B
    f32, bf16 = jnp.float32, jnp.bfloat16
    part = VMEM((half, DK, DK), f32)
    whole = VMEM((2 * half, DK, DK), f32)
    sems = lambda *shape: pltpu.SemaphoreType.DMA(shape)
    result = pl.pallas_call(
        functools.partial(layer_kernel, A, B),
        out_shape=jax.ShapeDtypeStruct((rows, width), bf16),
        in_specs=[smem, smem, vmem, vmem, vmem, anywhere, anywhere],
        out_specs=vmem,
        scratch_shapes=[
            VMEM((rows, width), bf16), VMEM((2,) + cache_state.shape, f32), VMEM((rows, width), bf16),
            VMEM((rows, width), bf16), VMEM((rows, width), f32), whole, whole,
            VMEM((rows, rows), f32), VMEM((prompts, rows, DK), bf16), VMEM((rows, DK), bf16),
            part, part, VMEM((B - 1, half, DK, DK), f32), part, part, part,
            sems(half), sems(half), sems(B - 1, 2 * half), sems(B - 1, 2 * half),
            sems(2 * half), sems(2 * half), sems(2 * half), sems(2 * half),
            sems(half), sems(half), pltpu.SemaphoreType.DMA, pltpu.SemaphoreType.DMA,
        ],
        compiler_params=pltpu.CompilerParams(collective_id=0, has_side_effects=True),
        name="layer",
    )(
        new_lengths, prefix_lengths, key_vectors, value_vectors, out_gain[None, :],
        queries, cache_state,
    )
    return pl.pallas_call(
        deliver_kernel,
        out_shape=jax.ShapeDtypeStruct((rows, width), bf16),
        in_specs=[anywhere],
        out_specs=anywhere,
        scratch_shapes=[VMEM((rows, width), bf16), sems(4), sems(4)],
        name="deliver",
    )(result)


def solution(mesh):
    in_specs = (
        P(("groups", "seq", "inner"), None),
        P(("groups", "seq", "inner"), None),
        P(("groups", "seq", "inner"), None),
        P("groups", "inner", None, None),
        P("groups"),
        P("groups"),
        P(),
    )
    out_specs = P(("groups", "seq", "inner"), None)
    return jax.shard_map(
        functools.partial(on_device, mesh.shape["seq"]),
        mesh=mesh, in_specs=in_specs, out_specs=out_specs, check_vma=False,
    )
```

```python
import functools
import math
import jax
import jax.numpy as jnp
from jax import lax
from jax.experimental import pallas as pl
from jax.experimental.pallas import tpu as pltpu
from jax.sharding import PartitionSpec as P

H = 16
DK = 128
VMEM = pltpu.VMEM
MESH = pl.DeviceIdType.MESH


def features(entries):
    values_f = entries.astype(jnp.float32)
    return jnp.where(values_f > 0, values_f + 1.0, jnp.exp(jnp.minimum(values_f, 0.0))).astype(
        jnp.bfloat16
    )


def prompt_starts(lengths_ref, prompts):
    starts, total = [], jnp.int32(0)
    for p in range(prompts):
        starts.append(total)
        total = total + lengths_ref[p]
    return starts


def no_start(starts, low, high):
    clear = jnp.float32(1.0)
    for start in starts:
        clear = clear * jnp.where((start >= low) & (start < high), 0.0, 1.0)
    return clear


def layer_kernel(
    A, B, lengths_ref, prefix_ref, k_ref, v_ref, gain_ref, q_hbm, cache_hbm, out_ref,
    q_ref, cached_ref, key_ref, carry_query_ref, acc_ref, own_ref, carry_ref, mask_ref,
    prompt_mask_ref, carry_mask_ref,
    pair_buf, x_buf, row_buf, z_in, z_out, back_buf,
    pair_s, pair_r, row_s, row_r, z_s, z_r, back_s, back_r, far_s, far_r, near_sem, q_sem,
):
    half = pair_buf.shape[0]
    rows = k_ref.shape[0]
    prompts = cached_ref.shape[1]
    chunk_rows = DK // 4
    s = lax.axis_index("seq")
    c = lax.axis_index("inner")
    other = 1 - c
    a, b = s // B, s % B
    first, last = a == 0, a == A - 1
    barrier = pltpu.get_barrier_semaphore()

    def greet(device):
        pl.semaphore_signal(barrier, inc=1, device_id=device, device_id_type=MESH)

    greet({"inner": other})
    mates = [a * B + (b + k) % B for k in range(1, B)]
    for mate in mates:
        greet({"seq": mate})
    pl.when(jnp.logical_not(first))(lambda: greet({"seq": s - B}))
    pl.when(jnp.logical_not(last))(lambda: greet({"seq": s + B}))

    def remote(src, dst, send, recv, device):
        return pltpu.make_async_remote_copy(
            src_ref=src, dst_ref=dst, send_sem=send, recv_sem=recv,
            device_id=device, device_id_type=MESH,
        )

    def pair(h):
        return remote(
            own_ref.at[other * half + h], pair_buf.at[h], pair_s.at[h], pair_r.at[h],
            {"inner": other},
        )

    def piece(ref, head, u):
        return ref.at[head, pl.ds(u * chunk_rows, chunk_rows)]

    def row(h, u):
        j = 4 * h + u
        return [
            remote(
                piece(x_buf, h, u), piece(row_buf.at[k], h, u), row_s.at[k, j], row_r.at[k, j],
                {"seq": mates[k]},
            )
            for k in range(B - 1)
        ]

    def down(h, u):
        j = 4 * h + u
        return remote(
            piece(z_out, h, u), piece(z_in, h, u), z_s.at[j], z_r.at[j],
            {"seq": jnp.minimum(s + B, A * B - 1)},
        )

    def back(h, u):
        j = 4 * h + u
        return remote(
            piece(back_buf, h, u), piece(carry_ref, c * half + h, u), back_s.at[j], back_r.at[j],
            {"inner": other},
        )

    near_copy = pltpu.make_async_copy(cache_hbm, cached_ref.at[0], near_sem)
    q_copy = pltpu.make_async_copy(q_hbm, q_ref, q_sem)

    def far(h):
        return remote(
            cache_hbm.at[:, h], cached_ref.at[1, :, h], far_s.at[h], far_r.at[h], {"inner": other}
        )

    q_copy.start()
    near_copy.start()

    starts = prompt_starts(lengths_ref, prompts)
    pair_rows = 2 * rows
    here = s * pair_rows
    first_row = here + c * rows
    row_begin, row_end = a * B * pair_rows, (a + 1) * B * pair_rows
    is_zero = jnp.where(c == 0, 1.0, 0.0).astype(jnp.float32)
    is_one = 1.0 - is_zero
    keep_zero = no_start(starts, here, here + rows)
    keep_one = no_start(starts, here + rows, here + pair_rows)
    mine_weight = is_one + is_zero * keep_one
    theirs_weight = is_zero + is_one * keep_one
    total_weights, prefix_weights = [], []
    for k in range(B):
        whose = (b + B - k) % B
        end = (a * B + whose + 1) * pair_rows
        total_weights.append(no_start(starts, end, row_end))
        prefix_weights.append(no_start(starts, end, here) * jnp.where(whose < b, 1.0, 0.0))
    keep_row = no_start(starts, row_begin, row_end)
    keep_prefix = no_start(starts, row_begin, here)

    last_start, first_start = jnp.int32(0), jnp.int32(0)
    for start in starts:
        last_start = jnp.maximum(last_start, jnp.where(start < first_row + rows, start, 0))
        first_start = jnp.maximum(first_start, jnp.where(start <= first_row, start, 0))
    column = lax.broadcasted_iota(jnp.int32, (rows, DK), 0) + first_row
    in_last = column >= last_start

    def columns(head):
        return pl.ds(pl.multiple_of(head * DK, DK), DK)

    def own_state(head):
        cols = columns(head)
        key_feat = features(k_ref[:, cols])
        key_ref[:, cols] = key_feat
        key_feat = jnp.where(in_last, key_feat, jnp.zeros_like(key_feat))
        own_ref[head] = lax.dot_general(
            key_feat, v_ref[:, cols], (((0,), (0,)), ((), ())), preferred_element_type=jnp.float32
        )

    def spread(h):
        pair(h).wait_recv()
        x_buf[h] = mine_weight * own_ref[c * half + h] + theirs_weight * pair_buf[h]
        for u in range(4):
            for copy in row(h, u):
                copy.start()

    own_state(other * half)
    ends = first.astype(jnp.int32) + last.astype(jnp.int32)
    pl.semaphore_wait(barrier, B + 2 - ends)
    pair(0).start()
    far(0).start()
    own_state(c * half)

    @pl.loop(1, half)
    def _(h):
        own_state(other * half + h)
        pair(h).start()
        far(h).start()
        own_state(c * half + h)
        spread(h - 1)

    spread(half - 1)

    @pl.when(first)
    def _():
        z_in[...] = jnp.zeros_like(z_in)

    segment_down = lax.broadcasted_iota(jnp.int32, (rows, rows), 0) + first_row
    segment_along = lax.broadcasted_iota(jnp.int32, (rows, rows), 1) + first_row
    mask = segment_down >= segment_along
    for start in starts:
        mask = mask & ((segment_down < start) | (segment_along >= start))
    mask_ref[...] = jnp.where(mask, 1.0, 0.0)
    for p in range(prompts):
        inside = column >= starts[p]
        if p + 1 < prompts:
            inside = inside & (column < starts[p + 1])
        prompt_mask_ref[p] = jnp.where(inside, 1.0, 0.0).astype(jnp.bfloat16)
    after = jnp.int32(2**31 - 1)
    for start in starts:
        after = jnp.minimum(after, jnp.where(start > first_row, start, after))
    carried = (column < after) & (first_start < first_row)
    carry_mask_ref[...] = jnp.where(carried, 1.0, 0.0).astype(jnp.bfloat16)
    near_copy.wait()
    q_copy.wait()

    def split(state):
        upper = state.astype(jnp.bfloat16)
        return upper, (state - upper.astype(jnp.float32)).astype(jnp.bfloat16)

    def local_terms(h, side):
        head = (other if side else c) * half + h
        cols = columns(head)
        query_feat = features(q_ref[:, cols])
        carry_query_ref[:, cols] = query_feat * carry_mask_ref[...]
        scores = lax.dot_general(
            query_feat, key_ref[:, cols], (((1,), (1,)), ((), ())),
            preferred_element_type=jnp.float32,
        )
        scores = (scores * mask_ref[...]).astype(jnp.bfloat16)
        acc = jnp.dot(scores, v_ref[:, cols], preferred_element_type=jnp.float32)
        uppers, lowers, queries = [], [], []
        for p in range(prompts):
            upper, lower = split(prefix_ref[p].astype(jnp.float32) * cached_ref[side, p, h])
            uppers.append(upper)
            lowers.append(lower)
            queries.append(query_feat * prompt_mask_ref[p])
        masked = jnp.concatenate(queries, axis=1)
        acc += jnp.dot(masked, jnp.concatenate(uppers, 0), preferred_element_type=jnp.float32)
        acc += jnp.dot(masked, jnp.concatenate(lowers, 0), preferred_element_type=jnp.float32)
        acc_ref[:, cols] = acc

    def finish(head):
        cols = columns(head)
        query = carry_query_ref[:, cols]
        state = jnp.concatenate(split(carry_ref[head]), axis=0)
        mixed = acc_ref[:, cols] + jnp.dot(
            jnp.concatenate([query, query], axis=1), state, preferred_element_type=jnp.float32
        )
        scale = 1.0 / jnp.sqrt(jnp.mean(mixed * mixed, axis=1, keepdims=True) + 1e-06)
        out_ref[:, cols] = (mixed * scale * gain_ref[:, cols]).astype(jnp.bfloat16)

    def both_local(h):
        far(h).wait_recv()
        local_terms(h, 0)
        local_terms(h, 1)

    def both_finish(h):
        for u in range(4):
            back(h, u).wait_recv()
        finish(c * half + h)
        finish(other * half + h)

    ahead = (half * a + A // 2) // max(A - 1, 1)
    late = a >= A // 2
    pl.loop(0, ahead)(both_local)

    @pl.loop(0, half)
    def _(h):
        for u in range(4):
            part = pl.ds(u * chunk_rows, chunk_rows)
            for copy in row(h, u):
                copy.wait_recv()
            total = total_weights[0] * x_buf[h, part]
            prefix = jnp.zeros_like(total)
            for k in range(1, B):
                got = row_buf[k - 1, h, part]
                total = total + total_weights[k] * got
                prefix = prefix + prefix_weights[k] * got
            pl.when(jnp.logical_not(first))(lambda: down(h, u).wait_recv())
            incoming = z_in[h, part]
            z_out[h, part] = total + keep_row * incoming
            pl.when(jnp.logical_not(last))(lambda: down(h, u).start())
            at_zero = prefix + keep_prefix * incoming
            mine, theirs = own_ref[c * half + h, part], pair_buf[h, part]
            at_one = is_zero * mine + is_one * theirs + keep_zero * at_zero
            back_buf[h, part] = is_one * at_zero + is_zero * at_one
            back(h, u).start()
            carry_ref[c * half + h, part] = is_zero * at_zero + is_one * at_one
        pl.when(late & (h >= ahead))(lambda: both_local(h))
        ready = ahead + h // 2
        early = jnp.logical_not(late) & (h % 2 == 1) & (ready < half)
        pl.when(early)(lambda: both_local(ready))
        pl.when(late & (h > 0))(lambda: both_finish(h - 1))

    pl.loop(jnp.where(late, half, jnp.minimum(ahead + half // 2, half)), half)(both_local)
    pl.loop(jnp.where(late, half - 1, 0), half)(both_finish)

    @pl.loop(0, half)
    def _(h):
        pair(h).wait_send()
        far(h).wait_send()
        for u in range(4):
            for copy in row(h, u):
                copy.wait_send()
            pl.when(jnp.logical_not(last))(lambda: down(h, u).wait_send())
            back(h, u).wait_send()


def deliver_kernel(in_hbm, out_hbm, buffer, in_sem, out_sem):
    pieces = in_sem.shape[0]
    size = buffer.shape[0] // pieces
    loads, stores = [], []
    for i in range(pieces):
        part = pl.ds(i * size, size)
        loads.append(pltpu.make_async_copy(in_hbm.at[part], buffer.at[part], in_sem.at[i]))
        stores.append(pltpu.make_async_copy(buffer.at[part], out_hbm.at[part], out_sem.at[i]))
    for load in loads:
        load.start()
    for load, store in zip(loads, stores):
        load.wait()
        store.start()
    for store in stores:
        store.wait()


def on_device(
    count, queries, key_vectors, value_vectors, cache_state, prefix_lengths, new_lengths, out_gain
):
    rows, width = queries.shape
    prompts, half = cache_state.shape[:2]
    vmem = pl.BlockSpec(memory_space=VMEM)
    smem = pl.BlockSpec(memory_space=pltpu.SMEM)
    anywhere = pl.BlockSpec(memory_space=pl.ANY)
    B = max(d for d in range(1, math.isqrt(count) + 1) if count % d == 0)
    A = count // B
    f32, bf16 = jnp.float32, jnp.bfloat16
    part = VMEM((half, DK, DK), f32)
    whole = VMEM((2 * half, DK, DK), f32)
    sems = lambda *shape: pltpu.SemaphoreType.DMA(shape)
    result = pl.pallas_call(
        functools.partial(layer_kernel, A, B),
        out_shape=jax.ShapeDtypeStruct((rows, width), bf16),
        in_specs=[smem, smem, vmem, vmem, vmem, anywhere, anywhere],
        out_specs=vmem,
        scratch_shapes=[
            VMEM((rows, width), bf16), VMEM((2,) + cache_state.shape, f32), VMEM((rows, width), bf16),
            VMEM((rows, width), bf16), VMEM((rows, width), f32), whole, whole,
            VMEM((rows, rows), f32), VMEM((prompts, rows, DK), bf16), VMEM((rows, DK), bf16),
            part, part, VMEM((B - 1, half, DK, DK), f32), part, part, part,
            sems(half), sems(half), sems(B - 1, 4 * half), sems(B - 1, 4 * half),
            sems(4 * half), sems(4 * half), sems(4 * half), sems(4 * half),
            sems(half), sems(half), pltpu.SemaphoreType.DMA, pltpu.SemaphoreType.DMA,
        ],
        compiler_params=pltpu.CompilerParams(collective_id=0, has_side_effects=True),
        name="layer",
    )(
        new_lengths, prefix_lengths, key_vectors, value_vectors, out_gain[None, :],
        queries, cache_state,
    )
    return pl.pallas_call(
        deliver_kernel,
        out_shape=jax.ShapeDtypeStruct((rows, width), bf16),
        in_specs=[anywhere],
        out_specs=anywhere,
        scratch_shapes=[VMEM((rows, width), bf16), sems(4), sems(4)],
        name="deliver",
    )(result)


def solution(mesh):
    in_specs = (
        P(("groups", "seq", "inner"), None),
        P(("groups", "seq", "inner"), None),
        P(("groups", "seq", "inner"), None),
        P("groups", "inner", None, None),
        P("groups"),
        P("groups"),
        P(),
    )
    out_specs = P(("groups", "seq", "inner"), None)
    return jax.shard_map(
        functools.partial(on_device, mesh.shape["seq"]),
        mesh=mesh, in_specs=in_specs, out_specs=out_specs, check_vma=False,
    )
```
